512 devices in a mesh: tiles: 512 (over y, z, x, core).
Axes of the slice: x: 4, y: 4, z: 16, core: 2. Of those that a mesh axis runs over, the one named last changes fastest.
Arguments:
- coords: float32 [2, 2097152], P(None, 'tiles'), may hold values from 0 to 16384, as said below
- field: float32 [64, 2097152], P(None, 'tiles'), may hold values from -11 to 11
- pair_tiles: int32 [2, 32768], P(None, 'tiles'), may hold values from -1 to 8191, as said below
- pair_count: int32 [512], P('tiles'), may hold values from 15 to 64, as said below
Outputs:
- solution: float32 [64, 2097152], P(None, 'tiles')
- residual: float32 [64, 2097152], P(None, 'tiles')
- direction: float32 [64, 2097152], P(None, 'tiles')
The draws below stay inside these ranges and needn't reach their ends.
Inputs may be any that keep to these rules, and one draw needn't show every extreme that they name: `coords`: tile t holds points t * 256 to (t + 1) * 256 - 1; device d holds tiles d * 16 to (d + 1) * 16 - 1. Any two points closer than 1 lie in one tile or in the two tiles of a live pair. `pair_tiles`: device d's slots are its 64 slots; its first pair_count[d] slots each hold a row tile A of device d and a column tile B with A < B <= A + 4 and B < 8192, no pair twice; its other slots hold -1 in both rows. `pair_count`: some device's count is 64 in every draw.
All inputs are finite; a program needn't handle non-finite values.
Results may differ from the reference program's by a relative error of at most 0.0003.
Values sent between devices are 32-bit elements; how exact they have to be, the bound alone decides.
A program may use at most 64 MiB of HBM per device.

```python
import jax
import jax.numpy as jnp
from jax import lax

TILE = 256
BAND = 4
TILES_DEV = 16
NRHS = 64
PAIR_CAP = 64
NTILES = 8192
NPTS = 2097152
PAIR_SLOTS = 32768
N_TILES = 512


widest = 8


def tile_layout(key):
    count = TILES_DEV * N_TILES
    widths = jax.random.randint(jax.random.fold_in(key, 101), (count,), 1, widest + 1)
    dense_device = jax.random.randint(jax.random.fold_in(key, 102), (), 0, N_TILES - 1)
    index = jnp.arange(count)
    low_tile = dense_device * TILES_DEV
    inside = (index >= low_tile) & (index < low_tile + TILES_DEV + BAND)
    widths = jnp.where(inside, 1, widths).astype(jnp.int32)
    starts = (jnp.cumsum(widths) - widths).astype(jnp.int32)
    return (widths, starts)


def pair_table(key):
    widths, starts = tile_layout(key)
    count = TILES_DEV * N_TILES
    row_ids = jnp.arange(count, dtype=jnp.int32)[:, None] + jnp.zeros((1, BAND), jnp.int32)
    col_ids = row_ids + jnp.arange(1, BAND + 1, dtype=jnp.int32)[None, :]
    safe_cols = jnp.minimum(col_ids, count - 1)
    gaps = starts[safe_cols] - starts[row_ids] - widths[row_ids]
    listed = (col_ids < count) & (gaps < BAND)
    listed = listed.reshape(N_TILES, PAIR_CAP)
    order = jnp.argsort(1 - listed.astype(jnp.int32), axis=1, stable=True)
    kept = jnp.take_along_axis(listed, order, axis=1)
    rows_sorted = jnp.take_along_axis(row_ids.reshape(N_TILES, PAIR_CAP), order, axis=1)
    cols_sorted = jnp.take_along_axis(col_ids.reshape(N_TILES, PAIR_CAP), order, axis=1)
    rows_out = jnp.where(kept, rows_sorted, -1).reshape(-1)
    cols_out = jnp.where(kept, cols_sorted, -1).reshape(-1)
    table = jnp.stack([rows_out, cols_out]).astype(jnp.int32)
    counts = jnp.sum(listed.astype(jnp.int32), axis=1).astype(jnp.int32)
    return (table, counts)


def draw_pair_tiles(key, part):
    return pair_table(key)[0]


def draw_pair_count(key, part):
    return pair_table(key)[1]


def draw_coords(key, part):
    widths, starts = tile_layout(key)
    across = jax.random.uniform(jax.random.fold_in(key, 201), (NTILES, TILE), jnp.float32)
    upward = jax.random.uniform(jax.random.fold_in(key, 202), (NTILES, TILE), jnp.float32)
    x_pos = (starts.astype(jnp.float32)[:, None] + across * widths.astype(jnp.float32)[:, None]) / BAND
    y_pos = upward
    return jnp.stack([x_pos.reshape(-1), y_pos.reshape(-1)]).astype(jnp.float32)


def draw_field(key, part):
    position = jnp.arange(NPTS).astype(jnp.float32) / NPTS
    ramp = jnp.sqrt(1.0 + 2.0 * position)
    noise = jnp.clip(jax.random.normal(jax.random.fold_in(key, 303), (NRHS, NPTS), jnp.float32), -6.0, 6.0)
    values = noise * ramp[None, :]
    return values.astype(jnp.float32)


def setup_inputs(seed: int = 0) -> dict:
    seeds = jax.random.split(jax.random.key(seed), 5)
    return {
        "coords": draw_coords(jax.random.fold_in(seeds[4], 71), 0),
        "field": draw_field(jax.random.fold_in(seeds[4], 71), 0),
        "pair_tiles": draw_pair_tiles(jax.random.fold_in(seeds[4], 71), 0),
        "pair_count": draw_pair_count(jax.random.fold_in(seeds[4], 71), 0),
    }


sill = 0.2
nugget = 1.0
tiny_square = 1e-12
highest = lax.Precision.HIGHEST

def wendland_tile(left_points, right_points):
    delta_x = left_points[0][:, None] - right_points[0][None, :]
    delta_y = left_points[1][:, None] - right_points[1][None, :]
    distance = jnp.sqrt(delta_x * delta_x + delta_y * delta_y + tiny_square)
    shell = jnp.maximum(1.0 - distance, 0.0)
    shell_sq = shell * shell
    return sill * shell_sq * shell_sq * (4.0 * distance + 1.0)

def apply_rows(values, kernel_tile):
    return lax.dot_general(values, kernel_tile, (((1,), (1,)), ((), ())), precision=highest, preferred_element_type=jnp.float32)

def apply_columns(values, kernel_tile):
    return jnp.dot(values, kernel_tile, precision=highest, preferred_element_type=jnp.float32)

def add_tile(totals, start, update):
    current = lax.dynamic_slice_in_dim(totals, start, TILE, 1)
    return lax.dynamic_update_slice_in_dim(totals, current + update, start, 1)

def reference(coords, field, pair_tiles, pair_count):
    columns = field.shape[0]
    points = coords.reshape(2, NTILES, TILE)
    values = field.reshape(columns, NTILES, TILE)

    def diagonal_one(tile_index):
        own_points = points[:, tile_index]
        return apply_rows(values[:, tile_index], wendland_tile(own_points, own_points))
    stacked = lax.map(diagonal_one, jnp.arange(NTILES).astype(jnp.int32))
    image = jnp.transpose(stacked, (1, 0, 2)).reshape(columns, NPTS)

    def pair_step(slot_index, totals):
        owner = slot_index // PAIR_CAP
        live = slot_index % PAIR_CAP < pair_count[owner]

        def include(totals):
            row_start = (pair_tiles[0, slot_index] * TILE).astype(jnp.int32)
            col_start = (pair_tiles[1, slot_index] * TILE).astype(jnp.int32)
            kernel_tile = wendland_tile(lax.dynamic_slice_in_dim(coords, row_start, TILE, 1), lax.dynamic_slice_in_dim(coords, col_start, TILE, 1))
            row_values = lax.dynamic_slice_in_dim(field, row_start, TILE, 1)
            col_values = lax.dynamic_slice_in_dim(field, col_start, TILE, 1)
            totals = add_tile(totals, row_start, apply_rows(col_values, kernel_tile))
            return add_tile(totals, col_start, apply_columns(row_values, kernel_tile))

        def keep_same(totals):
            return totals
        return lax.cond(live, include, keep_same, totals)
    image = lax.fori_loop(0, PAIR_SLOTS, pair_step, image)
    image = image + nugget * field
    start_sum = lax.optimization_barrier(jnp.sum(field * field, axis=1))
    curvature = lax.optimization_barrier(jnp.sum(field * image, axis=1))
    step_size = start_sum / curvature
    solution = step_size[:, None] * field
    residual = field - step_size[:, None] * image
    new_sum = lax.optimization_barrier(jnp.sum(residual * residual, axis=1))
    direction = residual + (new_sum / start_sum)[:, None] * field
    return (solution, residual, direction)
```

```python
import jax
import jax.numpy as jnp
from jax import lax
from jax.experimental import pallas as pl
from jax.experimental.pallas import tpu as pltpu
from jax.sharding import PartitionSpec as P

TILE = 256
BAND = 4
LANE = 128
CHUNK = 64
SILL = 0.2
NUGGET = 1.0
TINY = 16.0 * 1e-12
SCALE = SILL / 256.0
NX, NY, NZ, NC = 4, 4, 16, 2
PLANE = NX * NY * NC
EARLY = 6

f32 = jnp.float32
bf16 = jnp.bfloat16
NT = (((1,), (1,)), ((), ()))
NN = (((1,), (0,)), ((), ()))


def place(me):
    return me // (NZ * NX * NC), (me // (NX * NC)) % NZ, (me // NC) % NX, me % NC


def device(y, z, x, c):
    return (((y % NY) * NZ + z % NZ) * NX + x % NX) * NC + c % NC


def dot(a, b, dims):
    return lax.dot_general(a, b, dims, preferred_element_type=f32)


def lanes(first, count=1):
    return pl.ds(pl.multiple_of(first * LANE, LANE), count * LANE)


def covariance(xc, yc, xr, yr):
    dx = xc - xr
    dy = yc - yr
    q = dx * dx + dy * dy + TINY
    r = q * lax.rsqrt(q)
    s = jnp.maximum(4.0 - r, 0.0)
    s2 = s * s
    return s2 * s2 * (r + 1.0)


def split(v):
    high = v.astype(bf16)
    return high, (v - high.astype(f32)).astype(bf16)


def columns_of(cw, col, tile):
    for d in range(2):
        for h in range(2):
            row = cw[d : d + 1, lanes(tile * 2 + h)]
            col[d, h * LANE : (h + 1) * LANE, :] = jnp.broadcast_to(row, (LANE, LANE)).T


def strip_block(cw, col, kh, kl, tile, j):
    xr = cw[0:1, lanes(tile * 2 + j)]
    yr = cw[1:2, lanes(tile * 2 + j)]
    for g in range(0, TILE, CHUNK):
        rows = slice(g, g + CHUNK)
        high, low = split(covariance(col[0, rows, :], col[1, rows, :], xr, yr))
        kh[j, rows, :] = high
        kl[j, rows, :] = low


def both(v):
    half = v.shape[0] // 2
    return v[:half] + v[half:]


def row_apply(f2, acc, kh, kl, tile):
    width = 2 * (BAND + 1)
    values = [f2[tile * 2 + j] for j in range(width)]
    blocks = [k[j] for k in (kh, kl) for j in range(width)]
    out = dot(jnp.concatenate(values + values, 1), jnp.concatenate(blocks, 1), NT)
    acc[:, lanes(tile * 2, 2)] += both(out)


def col_apply(f2, acc, kh, kl, tile, b):
    values = [f2[tile * 2 + j] for j in range(2)]
    blocks = [jnp.concatenate([k[2 * b], k[2 * b + 1]], 1) for k in (kh, kl)]
    out = dot(jnp.concatenate(values + values, 1), jnp.concatenate(blocks, 0), NN)
    acc[:, lanes((tile + b) * 2, 2)] += both(out)


def order(step, late):
    return jnp.where(
        step < EARLY, step, jnp.where(step < EARLY + BAND, step + late - EARLY, step - BAND)
    )


def kernel(
    tiles,
    c_hbm,
    f_hbm,
    image_ref,
    step_ref,
    beta_ref,
    cw,
    fw,
    f2,
    acc,
    col0,
    col1,
    kh0,
    kl0,
    kh1,
    kl1,
    halo_c,
    halo_f,
    back,
    part,
    slots1,
    total1,
    slots2,
    load_sem,
    send_sem,
    recv_sem,
    near_sem,
    far_sem,
):
    n = f_hbm.shape[0]
    points = tiles * TILE
    rim = BAND * TILE
    me = lax.axis_index("tiles")
    count = NX * NY * NZ * NC
    y, z, x, c = place(me)
    right, left = (me + 1) % count, (me + count - 1) % count
    other = 1 - c

    load_f = pltpu.make_async_copy(f_hbm, fw, load_sem.at[0])
    load_c = pltpu.make_async_copy(c_hbm, cw.at[:, 0:points], load_sem.at[1])
    load_c.start()
    load_f.start()

    near = [left, right, device(y, z, x, other)]
    for dy, dz, dx in ((0, 0, 1), (0, 0, -1), (0, 1, 0), (0, -1, 0), (1, 0, 0), (-1, 0, 0)):
        for core in (c, other):
            near.append(device(y + dy, z + dz + NZ, x + dx + NX, core) if dy == 0 else device(y + dy + NY, z, x, core))
    barrier = pltpu.get_barrier_semaphore()
    for target in near:
        pl.semaphore_signal(barrier, inc=1, device_id=(target,))

    halo_copies = [
        pltpu.make_async_remote_copy(
            src_ref=src.at[:, 0:rim],
            dst_ref=dst,
            send_sem=send_sem.at[i],
            recv_sem=recv_sem.at[i],
            device_id=(left,),
        )
        for i, (src, dst) in enumerate(((c_hbm, halo_c), (f_hbm, halo_f)))
    ]
    back_copy = pltpu.make_async_remote_copy(
        src_ref=acc.at[:, points : points + rim],
        dst_ref=back,
        send_sem=send_sem.at[2],
        recv_sem=recv_sem.at[2],
        device_id=(right,),
    )

    def wait_near():
        pl.semaphore_wait(barrier, len(near))
        for copy in halo_copies:
            copy.start()
        for target in near:
            pl.semaphore_signal(near_sem, inc=1, device_id=(target,))

    spread = [device(y, z, x + 2, c), device(y + 2, z, x, c), device(y, z + 2, x, c), device(y, z + NZ - 2, x, c)]
    spread_far = [device(y, z + 4, x, c), device(y, z + NZ - 4, x, c)]

    def wait_two():
        pl.semaphore_wait(near_sem, len(near))
        for i, target in enumerate(spread):
            pl.semaphore_signal(far_sem.at[0], inc=1, device_id=(target,))

    def wait_four():
        pl.semaphore_wait(far_sem.at[0], len(spread))
        for target in spread_far:
            pl.semaphore_signal(far_sem.at[1], inc=1, device_id=(target,))

    def wait_eight():
        pl.semaphore_wait(far_sem.at[1], len(spread_far))

    acc[...] = jnp.zeros_like(acc)
    load_c.wait()
    cw[:, 0:points] = cw[:, 0:points] * 4.0
    columns_of(cw, col0, 0)
    columns_of(cw, col1, 1)
    wait_near()
    load_f.wait()

    @pl.loop(0, points // LANE)
    def _(j):
        high, low = split(fw[:, lanes(j)])
        f2[j, 0:n, :] = high
        f2[j, n : 2 * n, :] = low

    for j in range(2 * (BAND + 1)):
        strip_block(cw, col0, kh0, kl0, 0, j)

    late = tiles - BAND

    def half(kh, kl, kh_next, kl_next, col, col_next, now, following, after):
        for b in range(BAND + 1):
            for j in (2 * b, 2 * b + 1):
                strip_block(cw, col_next, kh_next, kl_next, following, j)
            if b == 0:
                columns_of(cw, col, after)
                row_apply(f2, acc, kh, kl, now)
            else:
                col_apply(f2, acc, kh, kl, now, b)

    last = tiles - 1

    @pl.loop(0, tiles // 2)
    def _(i):
        @pl.when(i == 1)
        def _():
            wait_two()

        @pl.when(i == 2)
        def _():
            wait_four()

        @pl.when(i == EARLY // 2 - 1)
        def _():
            for copy in halo_copies:
                copy.wait()
            cw[:, points : points + rim] = halo_c[...] * 4.0
            for j in range(rim // LANE):
                high, low = split(halo_f[:, j * LANE : (j + 1) * LANE])
                f2[points // LANE + j, 0:n, :] = high
                f2[points // LANE + j, n : 2 * n, :] = low

        @pl.when(i == (EARLY + BAND) // 2)
        def _():
            back_copy.start()
            wait_eight()

        s = i * 2
        places = [order(jnp.minimum(s + k, last), late) for k in range(4)]
        half(kh0, kl0, kh1, kl1, col0, col1, places[0], places[1], places[2])
        half(kh1, kl1, kh0, kl0, col1, col0, places[1], places[2], places[3])

    back_copy.wait()
    sums = [jnp.zeros((n, LANE), f32) for _ in range(3)]
    for j in range(points // LANE):
        at = slice(j * LANE, (j + 1) * LANE)
        field = fw[:, at]
        applied = acc[:, at]
        if j < rim // LANE:
            applied = applied + back[:, at]
        image = applied * SCALE + NUGGET * field
        image_ref[:, at] = image
        sums = [sums[0] + field * field, sums[1] + field * image, sums[2] + image * image]

    def over_lanes(v):
        return jnp.sum(v.T, axis=0, keepdims=True)

    mine = jnp.concatenate(
        [
            over_lanes(jnp.concatenate([sums[0], sums[1]], 0)),
            over_lanes(jnp.concatenate([sums[2], sums[2]], 0)),
        ],
        0,
    )

    def gather_sum(values, source, slots, here, members, sems):
        source[...] = values
        slots[here] = values
        copies = []
        for member, target in members:
            copies.append(
                pltpu.make_async_remote_copy(
                    src_ref=source,
                    dst_ref=slots.at[here],
                    send_sem=send_sem.at[sems],
                    recv_sem=recv_sem.at[sems],
                    device_id=(target,),
                )
            )
        for copy in copies:
            copy.start()
        others = slots.at[pl.ds(0, len(members))]
        pltpu.make_async_copy(others, others, recv_sem.at[sems]).wait()
        pltpu.make_async_copy(others, others, send_sem.at[sems]).wait()
        terms = [slots[k] for k in range(len(members) + 1)]
        while len(terms) > 1:
            terms = [a + b for a, b in zip(terms[::2], terms[1::2])]
        return terms[0]

    in_plane = (y * NX + x) * NC + c
    plane = []
    for k in range(1, PLANE):
        member = (in_plane + k) % PLANE
        plane.append((member, device(member // (NX * NC), z, (member // NC) % NX, member % NC)))
    total = gather_sum(mine, part, slots1, in_plane, plane, 3)
    line = []
    for k in range(1, NZ):
        line.append(((z + k) % NZ, device(y, z + k, x, c)))
    total = gather_sum(total, total1, slots2, z, line, 4)

    def columns(row):
        return jnp.broadcast_to(row, (LANE, LANE)).T

    first, second = columns(total[0:1]), columns(total[1:2])
    start_sum, curvature, square = first[:n], first[n:], second[:n]
    step = start_sum / curvature
    new_sum = start_sum - 2.0 * step * curvature + step * step * square
    step_ref[...] = step
    beta_ref[...] = new_sum / start_sum


def per_device(coords, field, pair_tiles, pair_count):
    n, points = field.shape
    tiles = points // TILE
    rim = BAND * TILE
    wide = points + rim
    vmem = pl.BlockSpec(memory_space=pltpu.VMEM)
    block = pltpu.VMEM((2 * (BAND + 1), TILE, LANE), bf16)
    image, step, beta = pl.pallas_call(
        lambda *refs: kernel(tiles, *refs),
        out_shape=(
            jax.ShapeDtypeStruct((n, points), f32),
            jax.ShapeDtypeStruct((n, LANE), f32),
            jax.ShapeDtypeStruct((n, LANE), f32),
        ),
        in_specs=[pl.BlockSpec(memory_space=pl.ANY)] * 2,
        out_specs=(vmem, vmem, vmem),
        scratch_shapes=[
            pltpu.VMEM((2, wide), f32),
            pltpu.VMEM((n, points), f32),
            pltpu.VMEM((wide // LANE, 2 * n, LANE), bf16),
            pltpu.VMEM((n, wide), f32),
            pltpu.VMEM((2, TILE, LANE), f32),
            pltpu.VMEM((2, TILE, LANE), f32),
            block,
            block,
            block,
            block,
            pltpu.VMEM((2, rim), f32),
            pltpu.VMEM((n, rim), f32),
            pltpu.VMEM((n, rim), f32),
            pltpu.VMEM((2, LANE), f32),
            pltpu.VMEM((PLANE, 2, LANE), f32),
            pltpu.VMEM((2, LANE), f32),
            pltpu.VMEM((NZ, 2, LANE), f32),
            pltpu.SemaphoreType.DMA((2,)),
            pltpu.SemaphoreType.DMA((5,)),
            pltpu.SemaphoreType.DMA((5,)),
            pltpu.SemaphoreType.REGULAR,
            pltpu.SemaphoreType.REGULAR((2,)),
        ],
        compiler_params=pltpu.CompilerParams(collective_id=0, has_side_effects=True),
        name="iterate",
    )(coords, field)
    step, beta = step[:, :1], beta[:, :1]
    residual = field - step * image
    return step * field, residual, residual + beta * field


def solution(mesh):
    return jax.shard_map(
        per_device,
        mesh=mesh,
        in_specs=(P(None, "tiles"), P(None, "tiles"), P(None, "tiles"), P("tiles")),
        out_specs=(P(None, "tiles"), P(None, "tiles"), P(None, "tiles")),
        check_vma=False,
    )
```

```python
import jax
import jax.numpy as jnp
from jax import lax
from jax.experimental import pallas as pl
from jax.experimental.pallas import tpu as pltpu
from jax.sharding import PartitionSpec as P

TILE = 256
BAND = 4
LANE = 128
CHUNK = 64
SILL = 0.2
NUGGET = 1.0
TINY = 16.0 * 1e-12
SCALE = SILL / 256.0
NX, NY, NZ, NC = 4, 4, 16, 2
PLANE = NX * NY * NC
PIECES = 4
GROUP = 4
EARLY = 8

f32 = jnp.float32
bf16 = jnp.bfloat16
NT = (((1,), (1,)), ((), ()))
NN = (((1,), (0,)), ((), ()))


def place(me):
    return me // (NZ * NX * NC), (me // (NX * NC)) % NZ, (me // NC) % NX, me % NC


def device(y, z, x, c):
    return (((y % NY) * NZ + z % NZ) * NX + x % NX) * NC + c % NC


def dot(a, b, dims):
    return lax.dot_general(a, b, dims, preferred_element_type=f32)


def lanes(first, count=1):
    return pl.ds(pl.multiple_of(first * LANE, LANE), count * LANE)


def covariance(xc, yc, xr, yr):
    dx = xc - xr
    dy = yc - yr
    q = dx * dx + dy * dy + TINY
    r = q * lax.rsqrt(q)
    s = jnp.maximum(4.0 - r, 0.0)
    s2 = s * s
    return s2 * s2 * (r + 1.0)


def split(v):
    high = v.astype(bf16)
    return high, (v - high.astype(f32)).astype(bf16)


def columns_of(cw, col, tile):
    for d in range(2):
        for h in range(2):
            row = cw[d : d + 1, lanes(tile * 2 + h)]
            col[d, h * LANE : (h + 1) * LANE, :] = jnp.broadcast_to(row, (LANE, LANE)).T


def block(cw, col, tile, b):
    out = []
    for j in (2 * b, 2 * b + 1):
        xr = cw[0:1, lanes(tile * 2 + j)]
        yr = cw[1:2, lanes(tile * 2 + j)]
        parts = []
        for g in range(0, TILE, CHUNK):
            rows = slice(g, g + CHUNK)
            parts.append(split(covariance(col[0, rows, :], col[1, rows, :], xr, yr)))
        out.append([jnp.concatenate([p[i] for p in parts], 0) for i in (0, 1)])
    return [jnp.concatenate([out[0][i], out[1][i]], 1) for i in (0, 1)]


def both(v):
    half = v.shape[0] // 2
    return v[:half] + v[half:]


def row_apply(f2, acc, blocks, tile, b):
    values = [f2[(tile + b) * 2 + j] for j in range(2)]
    out = dot(jnp.concatenate(values + values, 1), jnp.concatenate(blocks, 1), NT)
    acc[:, lanes(tile * 2, 2)] += both(out)


def col_apply(f2, acc, blocks, tile, b):
    values = [f2[tile * 2 + j] for j in range(2)]
    out = dot(jnp.concatenate(values + values, 1), jnp.concatenate(blocks, 0), NN)
    acc[:, lanes((tile + b) * 2, 2)] += both(out)


def order(step, late):
    return jnp.where(
        step < EARLY, step, jnp.where(step < EARLY + BAND, step + late - EARLY, step - BAND)
    )


def kernel(
    tiles,
    c_hbm,
    f_hbm,
    fw,
    image_ref,
    step_ref,
    beta_ref,
    cw,
    f2,
    acc,
    col0,
    col1,
    halo_c,
    halo_f,
    back,
    part,
    slots1,
    total1,
    slots2,
    load_sem,
    send_sem,
    recv_sem,
    near_sem,
    far_sem,
):
    n = f_hbm.shape[0]
    points = tiles * TILE
    rim = BAND * TILE
    me = lax.axis_index("tiles")
    count = NX * NY * NZ * NC
    y, z, x, c = place(me)
    right, left = (me + 1) % count, (me + count - 1) % count
    other = 1 - c

    load_f = pltpu.make_async_copy(f_hbm, fw, load_sem.at[0])
    load_c = pltpu.make_async_copy(c_hbm, cw.at[:, 0:points], load_sem.at[1])
    load_c.start()
    load_f.start()

    near = [left, right, device(y, z, x, other)]
    for dy, dz, dx in ((0, 0, 1), (0, 0, -1), (0, 1, 0), (0, -1, 0), (1, 0, 0), (-1, 0, 0)):
        for core in (c, other):
            near.append(device(y + dy, z + dz + NZ, x + dx + NX, core) if dy == 0 else device(y + dy + NY, z, x, core))
    barrier = pltpu.get_barrier_semaphore()
    for target in near:
        pl.semaphore_signal(barrier, inc=1, device_id=(target,))

    halo_copies = [
        pltpu.make_async_remote_copy(
            src_ref=src.at[:, 0:rim],
            dst_ref=dst,
            send_sem=send_sem.at[i],
            recv_sem=recv_sem.at[i],
            device_id=(left,),
        )
        for i, (src, dst) in enumerate(((c_hbm, halo_c), (f_hbm, halo_f)))
    ]
    back_copy = pltpu.make_async_remote_copy(
        src_ref=acc.at[:, points : points + rim],
        dst_ref=back,
        send_sem=send_sem.at[2],
        recv_sem=recv_sem.at[2],
        device_id=(right,),
    )

    def wait_near():
        pl.semaphore_wait(barrier, len(near))
        for copy in halo_copies:
            copy.start()
        for target in near:
            pl.semaphore_signal(near_sem, inc=1, device_id=(target,))

    spread = [device(y, z, x + 2, c), device(y + 2, z, x, c), device(y, z + 2, x, c), device(y, z + NZ - 2, x, c)]
    spread_far = [device(y, z + 4, x, c), device(y, z + NZ - 4, x, c)]

    def wait_two():
        pl.semaphore_wait(near_sem, len(near))
        for i, target in enumerate(spread):
            pl.semaphore_signal(far_sem.at[0], inc=1, device_id=(target,))

    def wait_four():
        pl.semaphore_wait(far_sem.at[0], len(spread))
        for target in spread_far:
            pl.semaphore_signal(far_sem.at[1], inc=1, device_id=(target,))

    def wait_eight():
        pl.semaphore_wait(far_sem.at[1], len(spread_far))

    acc[...] = jnp.zeros_like(acc)
    load_c.wait()
    cw[:, 0:points] = cw[:, 0:points] * 4.0
    columns_of(cw, col0, 0)
    cols = (col0, col1)
    load_f.wait()
    for j in range(points // LANE):
        high, low = split(fw[:, j * LANE : (j + 1) * LANE])
        f2[j, 0:n, :] = high
        f2[j, n : 2 * n, :] = low
    wait_near()

    late = tiles - BAND

    last = tiles - 1

    @pl.loop(0, tiles // GROUP)
    def _(i):
        @pl.when(i == 1)
        def _():
            wait_two()

        @pl.when(i == EARLY // GROUP)
        def _():
            wait_four()
            for copy in halo_copies:
                copy.wait()
            cw[:, points : points + rim] = halo_c[...] * 4.0
            for j in range(rim // LANE):
                high, low = split(halo_f[:, j * LANE : (j + 1) * LANE])
                f2[points // LANE + j, 0:n, :] = high
                f2[points // LANE + j, n : 2 * n, :] = low

        @pl.when(i == (EARLY + BAND) // GROUP)
        def _():
            back_copy.start()
            wait_eight()

        places = [order(jnp.minimum(i * GROUP + k, last), late) for k in range(GROUP + 1)]
        for g in range(GROUP):
            now, following = places[g], places[g + 1]
            for b in range(BAND + 1):
                blocks = block(cw, cols[g % 2], now, b)
                row_apply(f2, acc, blocks, now, b)
                if b == 0:
                    columns_of(cw, cols[(g + 1) % 2], following)
                else:
                    col_apply(f2, acc, blocks, now, b)

    sums = [jnp.zeros((n, LANE), f32) for _ in range(3)]
    for j in [*range(rim // LANE, points // LANE), *range(rim // LANE)]:
        if j == 0:
            back_copy.wait()
        at = slice(j * LANE, (j + 1) * LANE)
        field = fw[:, at]
        applied = acc[:, at]
        if j < rim // LANE:
            applied = applied + back[:, at]
        image = applied * SCALE + NUGGET * field
        image_ref[:, at] = image
        sums = [sums[0] + field * field, sums[1] + field * image, sums[2] + image * image]

    def over_lanes(v):
        return jnp.sum(v.T, axis=0, keepdims=True)

    mine = jnp.concatenate(
        [
            over_lanes(jnp.concatenate([sums[0], sums[1]], 0)),
            over_lanes(jnp.concatenate([sums[2], sums[2]], 0)),
        ],
        0,
    )

    def gather_sum(values, source, slots, here, members, sems):
        source[...] = values
        slots[here] = values
        copies = []
        for member, target in members:
            copies.append(
                pltpu.make_async_remote_copy(
                    src_ref=source,
                    dst_ref=slots.at[here],
                    send_sem=send_sem.at[sems],
                    recv_sem=recv_sem.at[sems],
                    device_id=(target,),
                )
            )
        for copy in copies:
            copy.start()
        others = slots.at[pl.ds(0, len(members))]
        pltpu.make_async_copy(others, others, recv_sem.at[sems]).wait()
        pltpu.make_async_copy(others, others, send_sem.at[sems]).wait()
        terms = [slots[k] for k in range(len(members) + 1)]
        while len(terms) > 1:
            terms = [a + b for a, b in zip(terms[::2], terms[1::2])]
        return terms[0]

    in_plane = (y * NX + x) * NC + c
    plane = []
    for dy, dx, core in sorted(
        ((a, b, e) for a in range(NY) for b in range(NX) for e in range(NC)),
        key=lambda m: -(min(m[0], NY - m[0]) + min(m[1], NX - m[1]) + m[2]),
    ):
        if (dy, dx, core) != (0, 0, 0):
            at = ((y + dy) % NY, (x + dx) % NX, (c + core) % NC)
            plane.append(((at[0] * NX + at[1]) * NC + at[2], device(at[0], z, at[1], at[2])))
    total = gather_sum(mine, part, slots1, in_plane, plane, 3)
    line = []
    for k in sorted(range(1, NZ), key=lambda k: -min(k, NZ - k)):
        line.append(((z + k) % NZ, device(y, z + k, x, c)))
    total = gather_sum(total, total1, slots2, z, line, 4)

    def columns(row):
        return jnp.broadcast_to(row, (LANE, LANE)).T

    first, second = columns(total[0:1]), columns(total[1:2])
    start_sum, curvature, square = first[:n], first[n:], second[:n]
    step = start_sum / curvature
    new_sum = start_sum - 2.0 * step * curvature + step * step * square
    step_ref[...] = step
    beta_ref[...] = new_sum / start_sum


def finish(field_ref, image_ref, step_ref, beta_ref, solution_hbm, residual_hbm, direction_hbm, made, sem):
    points = field_ref.shape[1]
    size = points // PIECES
    step, beta = step_ref[...], beta_ref[...]
    copies = []
    for p in range(PIECES):
        for j in range(p * size, (p + 1) * size, LANE):
            at = slice(j, j + LANE)
            field = field_ref[:, at]
            residual = field - step * image_ref[:, at]
            made[0, :, at] = step * field
            made[1, :, at] = residual
            made[2, :, at] = residual + beta * field
        at = slice(p * size, (p + 1) * size)
        for i, ref in enumerate((solution_hbm, residual_hbm, direction_hbm)):
            copy = pltpu.make_async_copy(made.at[i, :, at], ref.at[:, at], sem.at[i, p])
            copy.start()
            copies.append(copy)
    for copy in copies:
        copy.wait()


def per_device(coords, field, pair_tiles, pair_count):
    n, points = field.shape
    tiles = points // TILE
    rim = BAND * TILE
    wide = points + rim
    vmem = pl.BlockSpec(memory_space=pltpu.VMEM)
    whole, column = pltpu.VMEM((n, points), f32), pltpu.VMEM((n, LANE), f32)
    kept = pl.pallas_call(
        lambda *refs: kernel(tiles, *refs),
        out_shape=(whole, whole, column, column),
        in_specs=[pl.BlockSpec(memory_space=pl.ANY)] * 2,
        out_specs=(vmem,) * 4,
        scratch_shapes=[
            pltpu.VMEM((2, wide), f32),
            pltpu.VMEM((wide // LANE, 2 * n, LANE), bf16),
            pltpu.VMEM((n, wide), f32),
            pltpu.VMEM((2, TILE, LANE), f32),
            pltpu.VMEM((2, TILE, LANE), f32),
            pltpu.VMEM((2, rim), f32),
            pltpu.VMEM((n, rim), f32),
            pltpu.VMEM((n, rim), f32),
            pltpu.VMEM((2, LANE), f32),
            pltpu.VMEM((PLANE, 2, LANE), f32),
            pltpu.VMEM((2, LANE), f32),
            pltpu.VMEM((NZ, 2, LANE), f32),
            pltpu.SemaphoreType.DMA((2,)),
            pltpu.SemaphoreType.DMA((5,)),
            pltpu.SemaphoreType.DMA((5,)),
            pltpu.SemaphoreType.REGULAR,
            pltpu.SemaphoreType.REGULAR((2,)),
        ],
        compiler_params=pltpu.CompilerParams(collective_id=0, has_side_effects=True),
        name="iterate",
    )(coords, field)
    return pl.pallas_call(
        finish,
        out_shape=(jax.ShapeDtypeStruct((n, points), f32),) * 3,
        in_specs=[vmem] * 4,
        out_specs=(pl.BlockSpec(memory_space=pl.ANY),) * 3,
        scratch_shapes=[pltpu.VMEM((3, n, points), f32), pltpu.SemaphoreType.DMA((3, PIECES))],
        name="finish",
    )(*(pltpu.with_memory_space_constraint(v, pltpu.VMEM) for v in kept))


def solution(mesh):
    return jax.shard_map(
        per_device,
        mesh=mesh,
        in_specs=(P(None, "tiles"), P(None, "tiles"), P(None, "tiles"), P("tiles")),
        out_specs=(P(None, "tiles"), P(None, "tiles"), P(None, "tiles")),
        check_vma=False,
    )
```

```python
import jax
import jax.numpy as jnp
from jax import lax
from jax.experimental import pallas as pl
from jax.experimental.pallas import tpu as pltpu
from jax.sharding import PartitionSpec as P

TILE = 256
BAND = 4
LANE = 128
CHUNK = 64
SILL = 0.2
NUGGET = 1.0
TINY = 16.0 * 1e-12
SCALE = SILL / 256.0
NX, NY, NZ, NC = 4, 4, 16, 2
PLANE = NX * NY * NC
PIECES = 4
GROUP = 4
EARLY = 4

f32 = jnp.float32
bf16 = jnp.bfloat16
NT = (((1,), (1,)), ((), ()))
NN = (((1,), (0,)), ((), ()))


def place(me):
    return me // (NZ * NX * NC), (me // (NX * NC)) % NZ, (me // NC) % NX, me % NC


def device(y, z, x, c):
    return (((y % NY) * NZ + z % NZ) * NX + x % NX) * NC + c % NC


def dot(a, b, dims):
    return lax.dot_general(a, b, dims, preferred_element_type=f32)


def lanes(first, count=1):
    return pl.ds(pl.multiple_of(first * LANE, LANE), count * LANE)


def covariance(xc, yc, xr, yr):
    dx = xc - xr
    dy = yc - yr
    q = dx * dx + dy * dy + TINY
    r = q * lax.rsqrt(q)
    s = jnp.maximum(4.0 - r, 0.0)
    s2 = s * s
    return s2 * s2 * (r + 1.0)


def split(v):
    high = v.astype(bf16)
    return high, (v - high.astype(f32)).astype(bf16)


def columns_of(cw, col, tile):
    for d in range(2):
        for h in range(2):
            row = cw[d : d + 1, lanes(tile * 2 + h)]
            col[d, h * LANE : (h + 1) * LANE, :] = jnp.broadcast_to(row, (LANE, LANE)).T


def part(cw, col, tile, j, halves):
    xr = cw[0:1, lanes(tile * 2 + j)]
    yr = cw[1:2, lanes(tile * 2 + j)]
    parts = []
    for h in halves:
        for g in range(h * LANE, (h + 1) * LANE, CHUNK):
            rows = slice(g, g + CHUNK)
            parts.append(split(covariance(col[0, rows, :], col[1, rows, :], xr, yr)))
    return [jnp.concatenate([p[i] for p in parts], 0) for i in (0, 1)]


def block(cw, col, tile, b):
    left, right = [part(cw, col, tile, 2 * b + j, (0, 1)) for j in (0, 1)]
    return [jnp.concatenate([left[i], right[i]], 1) for i in (0, 1)]


def diagonal(cw, col, f2, acc, tile):
    first = part(cw, col, tile, 0, (0,))
    upper = part(cw, col, tile, 1, (0,))
    last = part(cw, col, tile, 1, (1,))
    values = [f2[tile * 2 + j] for j in range(2)]
    values = jnp.concatenate(values + values, 1)
    rows = [jnp.concatenate([first[i], upper[i]], 1) for i in (0, 1)]
    cols = [jnp.concatenate([upper[i], last[i]], 0) for i in (0, 1)]
    acc[:, lanes(tile * 2)] += both(dot(values, jnp.concatenate(rows, 1), NT))
    acc[:, lanes(tile * 2 + 1)] += both(dot(values, jnp.concatenate(cols, 0), NN))


def both(v):
    half = v.shape[0] // 2
    return v[:half] + v[half:]


def row_apply(f2, acc, blocks, tile, b):
    values = [f2[(tile + b) * 2 + j] for j in range(2)]
    out = dot(jnp.concatenate(values + values, 1), jnp.concatenate(blocks, 1), NT)
    acc[:, lanes(tile * 2, 2)] += both(out)


def col_apply(f2, acc, blocks, tile, b):
    values = [f2[tile * 2 + j] for j in range(2)]
    out = dot(jnp.concatenate(values + values, 1), jnp.concatenate(blocks, 0), NN)
    acc[:, lanes((tile + b) * 2, 2)] += both(out)


def order(step, late):
    return jnp.where(
        step < EARLY, step, jnp.where(step < EARLY + BAND, step + late - EARLY, step - BAND)
    )


def kernel(
    tiles,
    c_hbm,
    f_hbm,
    fw,
    image_ref,
    step_ref,
    beta_ref,
    cw,
    f2,
    acc,
    col0,
    col1,
    halo_c,
    halo_f,
    back,
    mine_ref,
    slots1,
    total1,
    slots2,
    load_sem,
    send_sem,
    recv_sem,
    near_sem,
    far_sem,
):
    n = f_hbm.shape[0]
    points = tiles * TILE
    rim = BAND * TILE
    me = lax.axis_index("tiles")
    count = NX * NY * NZ * NC
    y, z, x, c = place(me)
    right, left = (me + 1) % count, (me + count - 1) % count
    other = 1 - c

    load_c = pltpu.make_async_copy(c_hbm, cw.at[:, 0:points], load_sem.at[0])
    load_c.start()
    first = (GROUP + BAND) * TILE
    spans = ((0, first), (first, points))
    load_f = []
    for i, (begin, end) in enumerate(spans):
        at = slice(begin, end)
        load_f.append(pltpu.make_async_copy(f_hbm.at[:, at], fw.at[:, at], load_sem.at[1 + i]))
        load_f[-1].start()

    near = [left, right, device(y, z, x, other)]
    for dy, dz, dx in ((0, 0, 1), (0, 0, -1), (0, 1, 0), (0, -1, 0), (1, 0, 0), (-1, 0, 0)):
        for core in (c, other):
            near.append(device(y + dy, z + dz + NZ, x + dx + NX, core) if dy == 0 else device(y + dy + NY, z, x, core))
    barrier = pltpu.get_barrier_semaphore()
    for target in near:
        pl.semaphore_signal(barrier, inc=1, device_id=(target,))

    halo_copies = [
        pltpu.make_async_remote_copy(
            src_ref=src.at[:, 0:rim],
            dst_ref=dst,
            send_sem=send_sem.at[i],
            recv_sem=recv_sem.at[i],
            device_id=(left,),
        )
        for i, (src, dst) in enumerate(((c_hbm, halo_c), (f_hbm, halo_f)))
    ]
    back_copy = pltpu.make_async_remote_copy(
        src_ref=acc.at[:, points : points + rim],
        dst_ref=back,
        send_sem=send_sem.at[2],
        recv_sem=recv_sem.at[2],
        device_id=(right,),
    )

    def wait_near():
        pl.semaphore_wait(barrier, len(near))
        for copy in halo_copies:
            copy.start()
        for target in near:
            pl.semaphore_signal(near_sem, inc=1, device_id=(target,))

    spread = [device(y, z, x + 2, c), device(y + 2, z, x, c), device(y, z + 2, x, c), device(y, z + NZ - 2, x, c)]
    spread_far = [device(y, z + 4, x, c), device(y, z + NZ - 4, x, c)]

    def wait_two():
        pl.semaphore_wait(near_sem, len(near))
        for i, target in enumerate(spread):
            pl.semaphore_signal(far_sem.at[0], inc=1, device_id=(target,))

    def wait_four():
        pl.semaphore_wait(far_sem.at[0], len(spread))
        for target in spread_far:
            pl.semaphore_signal(far_sem.at[1], inc=1, device_id=(target,))

    def wait_eight():
        pl.semaphore_wait(far_sem.at[1], len(spread_far))

    acc[...] = jnp.zeros_like(acc)
    load_c.wait()
    cw[:, 0:points] = cw[:, 0:points] * 4.0
    columns_of(cw, col0, 0)
    cols = (col0, col1)
    wait_near()

    def take(span):
        begin, end = spans[span]
        load_f[span].wait()
        for j in range(begin // LANE, end // LANE):
            high, low = split(fw[:, j * LANE : (j + 1) * LANE])
            f2[j, 0:n, :] = high
            f2[j, n : 2 * n, :] = low

    take(0)

    late = tiles - BAND

    last = tiles - 1

    @pl.loop(0, tiles // GROUP)
    def _(i):
        @pl.when(i == 1)
        def _():
            take(1)
            wait_two()

        @pl.when(i == EARLY // GROUP)
        def _():
            for copy in halo_copies:
                copy.wait()
            cw[:, points : points + rim] = halo_c[...] * 4.0
            for j in range(rim // LANE):
                high, low = split(halo_f[:, j * LANE : (j + 1) * LANE])
                f2[points // LANE + j, 0:n, :] = high
                f2[points // LANE + j, n : 2 * n, :] = low

        @pl.when(i == (EARLY + BAND) // GROUP)
        def _():
            back_copy.start()
            wait_four()

        places = [order(jnp.minimum(i * GROUP + k, last), late) for k in range(GROUP + 1)]
        for g in range(GROUP):
            now, following = places[g], places[g + 1]
            for b in (*range(1, BAND + 1), 0):
                if b == 0:
                    diagonal(cw, cols[g % 2], f2, acc, now)
                    columns_of(cw, cols[(g + 1) % 2], following)
                    continue
                blocks = block(cw, cols[g % 2], now, b)
                row_apply(f2, acc, blocks, now, b)
                col_apply(f2, acc, blocks, now, b)

    sums = [jnp.zeros((n, LANE), f32) for _ in range(3)]
    for j in [*range(rim // LANE, points // LANE), *range(rim // LANE)]:
        if j == 0:
            back_copy.wait()
        at = slice(j * LANE, (j + 1) * LANE)
        field = fw[:, at]
        applied = acc[:, at]
        if j < rim // LANE:
            applied = applied + back[:, at]
        image = applied * SCALE + NUGGET * field
        image_ref[:, at] = image
        sums = [sums[0] + field * field, sums[1] + field * image, sums[2] + image * image]

    def over_lanes(v):
        return jnp.sum(v.T, axis=0, keepdims=True)

    mine = jnp.concatenate(
        [
            over_lanes(jnp.concatenate([sums[0], sums[1]], 0)),
            over_lanes(jnp.concatenate([sums[2], sums[2]], 0)),
        ],
        0,
    )

    def gather_sum(values, source, slots, here, members, sems):
        source[...] = values
        slots[here] = values
        copies = []
        for member, target in members:
            copies.append(
                pltpu.make_async_remote_copy(
                    src_ref=source,
                    dst_ref=slots.at[here],
                    send_sem=send_sem.at[sems],
                    recv_sem=recv_sem.at[sems],
                    device_id=(target,),
                )
            )
        for copy in copies:
            copy.start()
        others = slots.at[pl.ds(0, len(members))]
        pltpu.make_async_copy(others, others, recv_sem.at[sems]).wait()
        pltpu.make_async_copy(others, others, send_sem.at[sems]).wait()
        terms = [slots[k] for k in range(len(members) + 1)]
        while len(terms) > 1:
            terms = [a + b for a, b in zip(terms[::2], terms[1::2])]
        return terms[0]

    in_plane = (y * NX + x) * NC + c
    plane = []
    for dy, dx, core in sorted(
        ((a, b, e) for a in range(NY) for b in range(NX) for e in range(NC)),
        key=lambda m: -(min(m[0], NY - m[0]) + min(m[1], NX - m[1]) + m[2]),
    ):
        if (dy, dx, core) != (0, 0, 0):
            at = ((y + dy) % NY, (x + dx) % NX, (c + core) % NC)
            plane.append(((at[0] * NX + at[1]) * NC + at[2], device(at[0], z, at[1], at[2])))
    total = gather_sum(mine, mine_ref, slots1, in_plane, plane, 3)
    line = []
    for k in sorted(range(1, NZ), key=lambda k: -min(k, NZ - k)):
        line.append(((z + k) % NZ, device(y, z + k, x, c)))
    wait_eight()
    total = gather_sum(total, total1, slots2, z, line, 4)

    def columns(row):
        return jnp.broadcast_to(row, (LANE, LANE)).T

    first, second = columns(total[0:1]), columns(total[1:2])
    start_sum, curvature, square = first[:n], first[n:], second[:n]
    step = start_sum / curvature
    new_sum = start_sum - 2.0 * step * curvature + step * step * square
    step_ref[...] = step
    beta_ref[...] = new_sum / start_sum


def finish(field_ref, image_ref, step_ref, beta_ref, solution_hbm, residual_hbm, direction_hbm, made, sem):
    points = field_ref.shape[1]
    size = points // PIECES
    step, beta = step_ref[...], beta_ref[...]
    copies = []
    for p in range(PIECES):
        for j in range(p * size, (p + 1) * size, LANE):
            at = slice(j, j + LANE)
            field = field_ref[:, at]
            residual = field - step * image_ref[:, at]
            made[0, :, at] = step * field
            made[1, :, at] = residual
            made[2, :, at] = residual + beta * field
        at = slice(p * size, (p + 1) * size)
        for i, ref in enumerate((solution_hbm, residual_hbm, direction_hbm)):
            copy = pltpu.make_async_copy(made.at[i, :, at], ref.at[:, at], sem.at[i, p])
            copy.start()
            copies.append(copy)
    for copy in copies:
        copy.wait()


def per_device(coords, field, pair_tiles, pair_count):
    n, points = field.shape
    tiles = points // TILE
    rim = BAND * TILE
    wide = points + rim
    vmem = pl.BlockSpec(memory_space=pltpu.VMEM)
    whole, column = pltpu.VMEM((n, points), f32), pltpu.VMEM((n, LANE), f32)
    kept = pl.pallas_call(
        lambda *refs: kernel(tiles, *refs),
        out_shape=(whole, whole, column, column),
        in_specs=[pl.BlockSpec(memory_space=pl.ANY)] * 2,
        out_specs=(vmem,) * 4,
        scratch_shapes=[
            pltpu.VMEM((2, wide), f32),
            pltpu.VMEM((wide // LANE, 2 * n, LANE), bf16),
            pltpu.VMEM((n, wide), f32),
            pltpu.VMEM((2, TILE, LANE), f32),
            pltpu.VMEM((2, TILE, LANE), f32),
            pltpu.VMEM((2, rim), f32),
            pltpu.VMEM((n, rim), f32),
            pltpu.VMEM((n, rim), f32),
            pltpu.VMEM((2, LANE), f32),
            pltpu.VMEM((PLANE, 2, LANE), f32),
            pltpu.VMEM((2, LANE), f32),
            pltpu.VMEM((NZ, 2, LANE), f32),
            pltpu.SemaphoreType.DMA((3,)),
            pltpu.SemaphoreType.DMA((5,)),
            pltpu.SemaphoreType.DMA((5,)),
            pltpu.SemaphoreType.REGULAR,
            pltpu.SemaphoreType.REGULAR((2,)),
        ],
        compiler_params=pltpu.CompilerParams(collective_id=0, has_side_effects=True),
        name="iterate",
    )(coords, field)
    return pl.pallas_call(
        finish,
        out_shape=(jax.ShapeDtypeStruct((n, points), f32),) * 3,
        in_specs=[vmem] * 4,
        out_specs=(pl.BlockSpec(memory_space=pl.ANY),) * 3,
        scratch_shapes=[pltpu.VMEM((3, n, points), f32), pltpu.SemaphoreType.DMA((3, PIECES))],
        name="finish",
    )(*(pltpu.with_memory_space_constraint(v, pltpu.VMEM) for v in kept))


def solution(mesh):
    return jax.shard_map(
        per_device,
        mesh=mesh,
        in_specs=(P(None, "tiles"), P(None, "tiles"), P(None, "tiles"), P("tiles")),
        out_specs=(P(None, "tiles"), P(None, "tiles"), P(None, "tiles")),
        check_vma=False,
    )
```

```python
import jax
import jax.numpy as jnp
from jax import lax
from jax.experimental import pallas as pl
from jax.experimental.pallas import tpu as pltpu
from jax.sharding import PartitionSpec as P

TILE = 256
BAND = 4
LANE = 128
CHUNK = 64
SILL = 0.2
NUGGET = 1.0
TINY = 16.0 * 1e-12
SCALE = SILL / 256.0
NX, NY, NZ, NC = 4, 4, 16, 2
PLANE = NX * NY * NC
PIECES = 4
GROUP = 4
ENDS = 2
EARLY = 6

f32 = jnp.float32
bf16 = jnp.bfloat16
NT = (((1,), (1,)), ((), ()))
NN = (((1,), (0,)), ((), ()))


def place(me):
    return me // (NZ * NX * NC), (me // (NX * NC)) % NZ, (me // NC) % NX, me % NC


def device(y, z, x, c):
    return (((y % NY) * NZ + z % NZ) * NX + x % NX) * NC + c % NC


def dot(a, b, dims):
    return lax.dot_general(a, b, dims, preferred_element_type=f32)


def lanes(first, count=1):
    return pl.ds(pl.multiple_of(first * LANE, LANE), count * LANE)


def covariance(xc, yc, xr, yr):
    dx = xc - xr
    dy = yc - yr
    q = dx * dx + dy * dy + TINY
    r = q * lax.rsqrt(q)
    s = jnp.maximum(4.0 - r, 0.0)
    s2 = s * s
    return s2 * s2 * (r + 1.0)


def split(v):
    high = v.astype(bf16)
    return high, (v - high.astype(f32)).astype(bf16)


def columns_of(cw, col, tile):
    for d in range(2):
        for h in range(2):
            row = cw[d : d + 1, lanes(tile * 2 + h)]
            col[d, h * LANE : (h + 1) * LANE, :] = jnp.broadcast_to(row, (LANE, LANE)).T


def part(cw, col, tile, j, halves):
    xr = cw[0:1, lanes(tile * 2 + j)]
    yr = cw[1:2, lanes(tile * 2 + j)]
    parts = []
    for h in halves:
        for g in range(h * LANE, (h + 1) * LANE, CHUNK):
            rows = slice(g, g + CHUNK)
            parts.append(split(covariance(col[0, rows, :], col[1, rows, :], xr, yr)))
    return [jnp.concatenate([p[i] for p in parts], 0) for i in (0, 1)]


def block(cw, col, tile, b):
    left, right = [part(cw, col, tile, 2 * b + j, (0, 1)) for j in (0, 1)]
    return [jnp.concatenate([left[i], right[i]], 1) for i in (0, 1)]


def diagonal(cw, col, f2, acc, tile):
    first = part(cw, col, tile, 0, (0,))
    upper = part(cw, col, tile, 1, (0,))
    last = part(cw, col, tile, 1, (1,))
    values = [f2[tile * 2 + j] for j in range(2)]
    values = jnp.concatenate(values + values, 1)
    rows = [jnp.concatenate([first[i], upper[i]], 1) for i in (0, 1)]
    cols = [jnp.concatenate([upper[i], last[i]], 0) for i in (0, 1)]
    acc[:, lanes(tile * 2)] += both(dot(values, jnp.concatenate(rows, 1), NT))
    acc[:, lanes(tile * 2 + 1)] += both(dot(values, jnp.concatenate(cols, 0), NN))


def both(v):
    half = v.shape[0] // 2
    return v[:half] + v[half:]


def row_apply(f2, acc, blocks, tile, b):
    values = [f2[(tile + b) * 2 + j] for j in range(2)]
    out = dot(jnp.concatenate(values + values, 1), jnp.concatenate(blocks, 1), NT)
    acc[:, lanes(tile * 2, 2)] += both(out)


def col_apply(f2, acc, blocks, tile, b):
    values = [f2[tile * 2 + j] for j in range(2)]
    out = dot(jnp.concatenate(values + values, 1), jnp.concatenate(blocks, 0), NN)
    acc[:, lanes((tile + b) * 2, 2)] += both(out)


def order(step, late):
    return jnp.where(
        step < EARLY, step, jnp.where(step < EARLY + BAND, step + late - EARLY, step - BAND)
    )


def kernel(
    tiles,
    c_hbm,
    f_hbm,
    fw,
    image_ref,
    step_ref,
    beta_ref,
    cw,
    f2,
    acc,
    col0,
    col1,
    halo_c,
    halo_f,
    back,
    mine_ref,
    slots1,
    total1,
    slots2,
    load_sem,
    send_sem,
    recv_sem,
    near_sem,
    far_sem,
):
    n = f_hbm.shape[0]
    points = tiles * TILE
    rim = BAND * TILE
    me = lax.axis_index("tiles")
    count = NX * NY * NZ * NC
    y, z, x, c = place(me)
    right, left = (me + 1) % count, (me + count - 1) % count
    other = 1 - c

    load_c = pltpu.make_async_copy(c_hbm, cw.at[:, 0:points], load_sem.at[0])
    load_c.start()
    first = (ENDS + BAND) * TILE
    spans = ((0, first), (first, points))
    load_f = []
    for i, (begin, end) in enumerate(spans):
        at = slice(begin, end)
        load_f.append(pltpu.make_async_copy(f_hbm.at[:, at], fw.at[:, at], load_sem.at[1 + i]))
        load_f[-1].start()

    near = [left, right, device(y, z, x, other)]
    for dy, dz, dx in ((0, 0, 1), (0, 0, -1), (0, 1, 0), (0, -1, 0), (1, 0, 0), (-1, 0, 0)):
        for core in (c, other):
            near.append(device(y + dy, z + dz + NZ, x + dx + NX, core) if dy == 0 else device(y + dy + NY, z, x, core))
    barrier = pltpu.get_barrier_semaphore()
    for target in near:
        pl.semaphore_signal(barrier, inc=1, device_id=(target,))

    halo_copies = [
        pltpu.make_async_remote_copy(
            src_ref=src.at[:, 0:rim],
            dst_ref=dst,
            send_sem=send_sem.at[i],
            recv_sem=recv_sem.at[i],
            device_id=(left,),
        )
        for i, (src, dst) in enumerate(((c_hbm, halo_c), (f_hbm, halo_f)))
    ]
    back_copy = pltpu.make_async_remote_copy(
        src_ref=acc.at[:, points : points + rim],
        dst_ref=back,
        send_sem=send_sem.at[2],
        recv_sem=recv_sem.at[2],
        device_id=(right,),
    )

    def wait_near():
        pl.semaphore_wait(barrier, len(near))
        for copy in halo_copies:
            copy.start()
        for target in near:
            pl.semaphore_signal(near_sem, inc=1, device_id=(target,))

    spread = [device(y, z, x + 2, c), device(y + 2, z, x, c), device(y, z + 2, x, c), device(y, z + NZ - 2, x, c)]
    spread_far = [device(y, z + 4, x, c), device(y, z + NZ - 4, x, c)]

    def wait_two():
        pl.semaphore_wait(near_sem, len(near))
        for i, target in enumerate(spread):
            pl.semaphore_signal(far_sem.at[0], inc=1, device_id=(target,))

    def wait_four():
        pl.semaphore_wait(far_sem.at[0], len(spread))
        for target in spread_far:
            pl.semaphore_signal(far_sem.at[1], inc=1, device_id=(target,))

    def wait_eight():
        pl.semaphore_wait(far_sem.at[1], len(spread_far))

    acc[...] = jnp.zeros_like(acc)
    load_c.wait()
    cw[:, 0:points] = cw[:, 0:points] * 4.0
    columns_of(cw, col0, 0)
    cols = (col0, col1)
    wait_near()

    def take(span):
        begin, end = spans[span]
        load_f[span].wait()
        for j in range(begin // LANE, end // LANE):
            high, low = split(fw[:, j * LANE : (j + 1) * LANE])
            f2[j, 0:n, :] = high
            f2[j, n : 2 * n, :] = low

    take(0)

    late = tiles - BAND

    last = tiles - 1

    def strips(start, number):
        places = [order(jnp.minimum(start + k, last), late) for k in range(number + 1)]
        for g in range(number):
            now, following = places[g], places[g + 1]
            for b in (*range(1, BAND + 1), 0):
                if b == 0:
                    diagonal(cw, cols[g % 2], f2, acc, now)
                    columns_of(cw, cols[(g + 1) % 2], following)
                    continue
                blocks = block(cw, cols[g % 2], now, b)
                row_apply(f2, acc, blocks, now, b)
                col_apply(f2, acc, blocks, now, b)

    strips(0, ENDS)

    @pl.loop(0, (tiles - 2 * ENDS) // GROUP)
    def _(i):
        start = ENDS + i * GROUP

        @pl.when(start == ENDS)
        def _():
            take(1)
            wait_two()

        @pl.when(start == EARLY)
        def _():
            for copy in halo_copies:
                copy.wait()
            cw[:, points : points + rim] = halo_c[...] * 4.0
            for j in range(rim // LANE):
                high, low = split(halo_f[:, j * LANE : (j + 1) * LANE])
                f2[points // LANE + j, 0:n, :] = high
                f2[points // LANE + j, n : 2 * n, :] = low

        @pl.when(start == EARLY + BAND)
        def _():
            back_copy.start()
            wait_four()

        strips(start, GROUP)

    strips(tiles - ENDS, ENDS)
    sums = [jnp.zeros((n, LANE), f32) for _ in range(3)]
    for j in [*range(rim // LANE, points // LANE), *range(rim // LANE)]:
        if j == 0:
            back_copy.wait()
        at = slice(j * LANE, (j + 1) * LANE)
        field = fw[:, at]
        applied = acc[:, at]
        if j < rim // LANE:
            applied = applied + back[:, at]
        image = applied * SCALE + NUGGET * field
        image_ref[:, at] = image
        sums = [sums[0] + field * field, sums[1] + field * image, sums[2] + image * image]

    def over_lanes(v):
        return jnp.sum(v.T, axis=0, keepdims=True)

    mine = jnp.concatenate(
        [
            over_lanes(jnp.concatenate([sums[0], sums[1]], 0)),
            over_lanes(jnp.concatenate([sums[2], sums[2]], 0)),
        ],
        0,
    )

    def gather_sum(values, source, slots, here, members, sems):
        source[...] = values
        slots[here] = values
        copies = []
        for member, target in members:
            copies.append(
                pltpu.make_async_remote_copy(
                    src_ref=source,
                    dst_ref=slots.at[here],
                    send_sem=send_sem.at[sems],
                    recv_sem=recv_sem.at[sems],
                    device_id=(target,),
                )
            )
        for copy in copies:
            copy.start()
        others = slots.at[pl.ds(0, len(members))]
        pltpu.make_async_copy(others, others, recv_sem.at[sems]).wait()
        pltpu.make_async_copy(others, others, send_sem.at[sems]).wait()
        terms = [slots[k] for k in range(len(members) + 1)]
        while len(terms) > 1:
            terms = [a + b for a, b in zip(terms[::2], terms[1::2])]
        return terms[0]

    in_plane = (y * NX + x) * NC + c
    plane = []
    for dy, dx, core in sorted(
        ((a, b, e) for a in range(NY) for b in range(NX) for e in range(NC)),
        key=lambda m: -(min(m[0], NY - m[0]) + min(m[1], NX - m[1]) + m[2]),
    ):
        if (dy, dx, core) != (0, 0, 0):
            at = ((y + dy) % NY, (x + dx) % NX, (c + core) % NC)
            plane.append(((at[0] * NX + at[1]) * NC + at[2], device(at[0], z, at[1], at[2])))
    total = gather_sum(mine, mine_ref, slots1, in_plane, plane, 3)
    line = []
    for k in sorted(range(1, NZ), key=lambda k: -min(k, NZ - k)):
        line.append(((z + k) % NZ, device(y, z + k, x, c)))
    wait_eight()
    total = gather_sum(total, total1, slots2, z, line, 4)

    def columns(row):
        return jnp.broadcast_to(row, (LANE, LANE)).T

    first, second = columns(total[0:1]), columns(total[1:2])
    start_sum, curvature, square = first[:n], first[n:], second[:n]
    step = start_sum / curvature
    new_sum = start_sum - 2.0 * step * curvature + step * step * square
    step_ref[...] = step
    beta_ref[...] = new_sum / start_sum


def finish(field_ref, image_ref, step_ref, beta_ref, solution_hbm, residual_hbm, direction_hbm, made, sem):
    points = field_ref.shape[1]
    size = points // PIECES
    step, beta = step_ref[...], beta_ref[...]
    copies = []
    for p in range(PIECES):
        for j in range(p * size, (p + 1) * size, LANE):
            at = slice(j, j + LANE)
            field = field_ref[:, at]
            residual = field - step * image_ref[:, at]
            made[0, :, at] = step * field
            made[1, :, at] = residual
            made[2, :, at] = residual + beta * field
        at = slice(p * size, (p + 1) * size)
        for i, ref in enumerate((solution_hbm, residual_hbm, direction_hbm)):
            copy = pltpu.make_async_copy(made.at[i, :, at], ref.at[:, at], sem.at[i, p])
            copy.start()
            copies.append(copy)
    for copy in copies:
        copy.wait()


def per_device(coords, field, pair_tiles, pair_count):
    n, points = field.shape
    tiles = points // TILE
    rim = BAND * TILE
    wide = points + rim
    vmem = pl.BlockSpec(memory_space=pltpu.VMEM)
    whole, column = pltpu.VMEM((n, points), f32), pltpu.VMEM((n, LANE), f32)
    kept = pl.pallas_call(
        lambda *refs: kernel(tiles, *refs),
        out_shape=(whole, whole, column, column),
        in_specs=[pl.BlockSpec(memory_space=pl.ANY)] * 2,
        out_specs=(vmem,) * 4,
        scratch_shapes=[
            pltpu.VMEM((2, wide), f32),
            pltpu.VMEM((wide // LANE, 2 * n, LANE), bf16),
            pltpu.VMEM((n, wide), f32),
            pltpu.VMEM((2, TILE, LANE), f32),
            pltpu.VMEM((2, TILE, LANE), f32),
            pltpu.VMEM((2, rim), f32),
            pltpu.VMEM((n, rim), f32),
            pltpu.VMEM((n, rim), f32),
            pltpu.VMEM((2, LANE), f32),
            pltpu.VMEM((PLANE, 2, LANE), f32),
            pltpu.VMEM((2, LANE), f32),
            pltpu.VMEM((NZ, 2, LANE), f32),
            pltpu.SemaphoreType.DMA((3,)),
            pltpu.SemaphoreType.DMA((5,)),
            pltpu.SemaphoreType.DMA((5,)),
            pltpu.SemaphoreType.REGULAR,
            pltpu.SemaphoreType.REGULAR((2,)),
        ],
        compiler_params=pltpu.CompilerParams(collective_id=0, has_side_effects=True),
        name="iterate",
    )(coords, field)
    return pl.pallas_call(
        finish,
        out_shape=(jax.ShapeDtypeStruct((n, points), f32),) * 3,
        in_specs=[vmem] * 4,
        out_specs=(pl.BlockSpec(memory_space=pl.ANY),) * 3,
        scratch_shapes=[pltpu.VMEM((3, n, points), f32), pltpu.SemaphoreType.DMA((3, PIECES))],
        name="finish",
    )(*(pltpu.with_memory_space_constraint(v, pltpu.VMEM) for v in kept))


def solution(mesh):
    return jax.shard_map(
        per_device,
        mesh=mesh,
        in_specs=(P(None, "tiles"), P(None, "tiles"), P(None, "tiles"), P("tiles")),
        out_specs=(P(None, "tiles"), P(None, "tiles"), P(None, "tiles")),
        check_vma=False,
    )
```

```python
import jax
import jax.numpy as jnp
from jax import lax
from jax.experimental import pallas as pl
from jax.experimental.pallas import tpu as pltpu
from jax.sharding import PartitionSpec as P

TILE = 256
BAND = 4
LANE = 128
CHUNK = 64
SILL = 0.2
NUGGET = 1.0
TINY = 16.0 * 1e-12
SCALE = SILL / 256.0
NX, NY, NZ, NC = 4, 4, 16, 2
PLANE = NX * NY * NC
PIECES = 4
GROUP = 4
ENDS = 2
EARLY = 6

f32 = jnp.float32
bf16 = jnp.bfloat16
NT = (((1,), (1,)), ((), ()))
NN = (((1,), (0,)), ((), ()))


def place(me):
    return me // (NZ * NX * NC), (me // (NX * NC)) % NZ, (me // NC) % NX, me % NC


def device(y, z, x, c):
    return (((y % NY) * NZ + z % NZ) * NX + x % NX) * NC + c % NC


def dot(a, b, dims):
    return lax.dot_general(a, b, dims, preferred_element_type=f32)


def lanes(first, count=1):
    return pl.ds(pl.multiple_of(first * LANE, LANE), count * LANE)


def covariance(xc, yc, xr, yr):
    dx = xc - xr
    dy = yc - yr
    q = dx * dx + dy * dy + TINY
    r = q * lax.rsqrt(q)
    s = jnp.maximum(4.0 - r, 0.0)
    s2 = s * s
    return s2 * s2 * (r + 1.0)


def split(v):
    high = v.astype(bf16)
    return high, (v - high.astype(f32)).astype(bf16)


def columns_of(cw, col, tile):
    for d in range(2):
        for h in range(2):
            row = cw[d : d + 1, lanes(tile * 2 + h)]
            col[d, h * LANE : (h + 1) * LANE, :] = jnp.broadcast_to(row, (LANE, LANE)).T


def part(cw, col, tile, j, halves):
    xr = cw[0:1, lanes(tile * 2 + j)]
    yr = cw[1:2, lanes(tile * 2 + j)]
    parts = []
    for h in halves:
        for g in range(h * LANE, (h + 1) * LANE, CHUNK):
            rows = slice(g, g + CHUNK)
            parts.append(split(covariance(col[0, rows, :], col[1, rows, :], xr, yr)))
    return [jnp.concatenate([p[i] for p in parts], 0) for i in (0, 1)]


def block(cw, col, tile, b):
    left, right = [part(cw, col, tile, 2 * b + j, (0, 1)) for j in (0, 1)]
    return [jnp.concatenate([left[i], right[i]], 1) for i in (0, 1)]


def diagonal(cw, col, f2, acc, tile):
    first = part(cw, col, tile, 0, (0,))
    upper = part(cw, col, tile, 1, (0,))
    last = part(cw, col, tile, 1, (1,))
    values = [f2[tile * 2 + j] for j in range(2)]
    values = jnp.concatenate(values + values, 1)
    rows = [jnp.concatenate([first[i], upper[i]], 1) for i in (0, 1)]
    cols = [jnp.concatenate([upper[i], last[i]], 0) for i in (0, 1)]
    acc[:, lanes(tile * 2)] += both(dot(values, jnp.concatenate(rows, 1), NT))
    acc[:, lanes(tile * 2 + 1)] += both(dot(values, jnp.concatenate(cols, 0), NN))


def both(v):
    half = v.shape[0] // 2
    return v[:half] + v[half:]


def row_apply(f2, acc, blocks, tile, b):
    values = [f2[(tile + b) * 2 + j] for j in range(2)]
    out = dot(jnp.concatenate(values + values, 1), jnp.concatenate(blocks, 1), NT)
    acc[:, lanes(tile * 2, 2)] += both(out)


def col_apply(f2, acc, blocks, tile, b):
    values = [f2[tile * 2 + j] for j in range(2)]
    out = dot(jnp.concatenate(values + values, 1), jnp.concatenate(blocks, 0), NN)
    acc[:, lanes((tile + b) * 2, 2)] += both(out)


def order(step, late):
    return jnp.where(
        step < EARLY, step, jnp.where(step < EARLY + BAND, step + late - EARLY, step - BAND)
    )


def kernel(
    tiles,
    c_hbm,
    f_hbm,
    fw,
    image_ref,
    step_ref,
    beta_ref,
    cw,
    f2,
    acc,
    col0,
    col1,
    halo_c,
    halo_f,
    back,
    mine_ref,
    slots1,
    total1,
    slots2,
    load_sem,
    send_sem,
    recv_sem,
    near_sem,
    far_sem,
):
    n = f_hbm.shape[0]
    points = tiles * TILE
    rim = BAND * TILE
    me = lax.axis_index("tiles")
    count = NX * NY * NZ * NC
    y, z, x, c = place(me)
    right, left = (me + 1) % count, (me + count - 1) % count
    other = 1 - c

    load_c = pltpu.make_async_copy(c_hbm, cw.at[:, 0:points], load_sem.at[0])
    load_c.start()
    first = (ENDS + BAND) * TILE
    spans = ((0, first), (first, points))
    load_f = []
    for i, (begin, end) in enumerate(spans):
        at = slice(begin, end)
        load_f.append(pltpu.make_async_copy(f_hbm.at[:, at], fw.at[:, at], load_sem.at[1 + i]))
        load_f[-1].start()

    near = [left, right, device(y, z, x, other)]
    for dy, dz, dx in ((0, 0, 1), (0, 0, -1), (0, 1, 0), (0, -1, 0), (1, 0, 0), (-1, 0, 0)):
        for core in (c, other):
            near.append(device(y + dy, z + dz + NZ, x + dx + NX, core) if dy == 0 else device(y + dy + NY, z, x, core))
    barrier = pltpu.get_barrier_semaphore()
    for target in near:
        pl.semaphore_signal(barrier, inc=1, device_id=(target,))

    halo_copies = [
        pltpu.make_async_remote_copy(
            src_ref=src.at[:, 0:rim],
            dst_ref=dst,
            send_sem=send_sem.at[i],
            recv_sem=recv_sem.at[i],
            device_id=(left,),
        )
        for i, (src, dst) in enumerate(((c_hbm, halo_c), (f_hbm, halo_f)))
    ]
    back_copy = pltpu.make_async_remote_copy(
        src_ref=acc.at[:, points : points + rim],
        dst_ref=back,
        send_sem=send_sem.at[2],
        recv_sem=recv_sem.at[2],
        device_id=(right,),
    )

    def wait_near():
        pl.semaphore_wait(barrier, len(near))
        for copy in halo_copies:
            copy.start()
        for target in near:
            pl.semaphore_signal(near_sem, inc=1, device_id=(target,))

    spread = [device(y, z, x + 2, c), device(y + 2, z, x, c), device(y, z + 2, x, c), device(y, z + NZ - 2, x, c)]
    spread_far = [device(y, z + 4, x, c), device(y, z + NZ - 4, x, c)]

    def wait_two():
        pl.semaphore_wait(near_sem, len(near))
        for i, target in enumerate(spread):
            pl.semaphore_signal(far_sem.at[0], inc=1, device_id=(target,))

    def wait_four():
        pl.semaphore_wait(far_sem.at[0], len(spread))
        for target in spread_far:
            pl.semaphore_signal(far_sem.at[1], inc=1, device_id=(target,))

    def wait_eight():
        pl.semaphore_wait(far_sem.at[1], len(spread_far))

    acc[...] = jnp.zeros_like(acc)
    load_c.wait()
    cw[:, 0:points] = cw[:, 0:points] * 4.0
    columns_of(cw, col0, 0)
    cols = (col0, col1)
    def take(span):
        begin, end = spans[span]
        load_f[span].wait()
        for j in range(begin // LANE, end // LANE):
            high, low = split(fw[:, j * LANE : (j + 1) * LANE])
            f2[j, 0:n, :] = high
            f2[j, n : 2 * n, :] = low

    take(0)

    late = tiles - BAND

    last = tiles - 1

    def strips(start, number, odd=0):
        places = [order(jnp.minimum(start + k, last), late) for k in range(number + 1)]
        for g in range(number):
            now, following = places[g], places[g + 1]
            for b in (*range(1, BAND + 1), 0):
                if b == 0:
                    diagonal(cw, cols[(odd + g) % 2], f2, acc, now)
                    columns_of(cw, cols[(odd + g + 1) % 2], following)
                    continue
                blocks = block(cw, cols[(odd + g) % 2], now, b)
                row_apply(f2, acc, blocks, now, b)
                col_apply(f2, acc, blocks, now, b)

    strips(0, 1)
    wait_near()
    strips(1, ENDS - 1, 1)

    @pl.loop(0, (tiles - 2 * ENDS) // GROUP)
    def _(i):
        start = ENDS + i * GROUP

        @pl.when(start == ENDS)
        def _():
            take(1)

        @pl.when(start == EARLY)
        def _():
            wait_two()
            for copy in halo_copies:
                copy.wait()
            cw[:, points : points + rim] = halo_c[...] * 4.0
            for j in range(rim // LANE):
                high, low = split(halo_f[:, j * LANE : (j + 1) * LANE])
                f2[points // LANE + j, 0:n, :] = high
                f2[points // LANE + j, n : 2 * n, :] = low

        @pl.when(start == EARLY + BAND)
        def _():
            back_copy.start()
            wait_four()

        strips(start, GROUP)

    strips(tiles - ENDS, ENDS)
    sums = [jnp.zeros((n, LANE), f32) for _ in range(3)]
    for j in [*range(rim // LANE, points // LANE), *range(rim // LANE)]:
        if j == 0:
            back_copy.wait()
        at = slice(j * LANE, (j + 1) * LANE)
        field = fw[:, at]
        applied = acc[:, at]
        if j < rim // LANE:
            applied = applied + back[:, at]
        image = applied * SCALE + NUGGET * field
        image_ref[:, at] = image
        sums = [sums[0] + field * field, sums[1] + field * image, sums[2] + image * image]

    def over_lanes(v):
        return jnp.sum(v.T, axis=0, keepdims=True)

    mine = jnp.concatenate(
        [
            over_lanes(jnp.concatenate([sums[0], sums[1]], 0)),
            over_lanes(jnp.concatenate([sums[2], sums[2]], 0)),
        ],
        0,
    )

    def gather_sum(values, source, slots, here, members, sems):
        source[...] = values
        slots[here] = values
        copies = []
        for member, target in members:
            copies.append(
                pltpu.make_async_remote_copy(
                    src_ref=source,
                    dst_ref=slots.at[here],
                    send_sem=send_sem.at[sems],
                    recv_sem=recv_sem.at[sems],
                    device_id=(target,),
                )
            )
        for copy in copies:
            copy.start()
        others = slots.at[pl.ds(0, len(members))]
        pltpu.make_async_copy(others, others, recv_sem.at[sems]).wait()
        pltpu.make_async_copy(others, others, send_sem.at[sems]).wait()
        terms = [slots[k] for k in range(len(members) + 1)]
        while len(terms) > 1:
            terms = [a + b for a, b in zip(terms[::2], terms[1::2])]
        return terms[0]

    in_plane = (y * NX + x) * NC + c
    plane = []
    for dy, dx, core in sorted(
        ((a, b, e) for a in range(NY) for b in range(NX) for e in range(NC)),
        key=lambda m: -(min(m[0], NY - m[0]) + min(m[1], NX - m[1]) + m[2]),
    ):
        if (dy, dx, core) != (0, 0, 0):
            at = ((y + dy) % NY, (x + dx) % NX, (c + core) % NC)
            plane.append(((at[0] * NX + at[1]) * NC + at[2], device(at[0], z, at[1], at[2])))
    total = gather_sum(mine, mine_ref, slots1, in_plane, plane, 3)
    line = []
    for k in sorted(range(1, NZ), key=lambda k: -min(k, NZ - k)):
        line.append(((z + k) % NZ, device(y, z + k, x, c)))
    wait_eight()
    total = gather_sum(total, total1, slots2, z, line, 4)

    def columns(row):
        return jnp.broadcast_to(row, (LANE, LANE)).T

    first, second = columns(total[0:1]), columns(total[1:2])
    start_sum, curvature, square = first[:n], first[n:], second[:n]
    step = start_sum / curvature
    new_sum = start_sum - 2.0 * step * curvature + step * step * square
    step_ref[...] = step
    beta_ref[...] = new_sum / start_sum


def finish(field_ref, image_ref, step_ref, beta_ref, solution_hbm, residual_hbm, direction_hbm, made, sem):
    points = field_ref.shape[1]
    size = points // PIECES
    step, beta = step_ref[...], beta_ref[...]
    copies = []
    for p in range(PIECES):
        for j in range(p * size, (p + 1) * size, LANE):
            at = slice(j, j + LANE)
            field = field_ref[:, at]
            residual = field - step * image_ref[:, at]
            made[0, :, at] = step * field
            made[1, :, at] = residual
            made[2, :, at] = residual + beta * field
        at = slice(p * size, (p + 1) * size)
        for i, ref in enumerate((solution_hbm, residual_hbm, direction_hbm)):
            copy = pltpu.make_async_copy(made.at[i, :, at], ref.at[:, at], sem.at[i, p])
            copy.start()
            copies.append(copy)
    for copy in copies:
        copy.wait()


def per_device(coords, field, pair_tiles, pair_count):
    n, points = field.shape
    tiles = points // TILE
    rim = BAND * TILE
    wide = points + rim
    vmem = pl.BlockSpec(memory_space=pltpu.VMEM)
    whole, column = pltpu.VMEM((n, points), f32), pltpu.VMEM((n, LANE), f32)
    kept = pl.pallas_call(
        lambda *refs: kernel(tiles, *refs),
        out_shape=(whole, whole, column, column),
        in_specs=[pl.BlockSpec(memory_space=pl.ANY)] * 2,
        out_specs=(vmem,) * 4,
        scratch_shapes=[
            pltpu.VMEM((2, wide), f32),
            pltpu.VMEM((wide // LANE, 2 * n, LANE), bf16),
            pltpu.VMEM((n, wide), f32),
            pltpu.VMEM((2, TILE, LANE), f32),
            pltpu.VMEM((2, TILE, LANE), f32),
            pltpu.VMEM((2, rim), f32),
            pltpu.VMEM((n, rim), f32),
            pltpu.VMEM((n, rim), f32),
            pltpu.VMEM((2, LANE), f32),
            pltpu.VMEM((PLANE, 2, LANE), f32),
            pltpu.VMEM((2, LANE), f32),
            pltpu.VMEM((NZ, 2, LANE), f32),
            pltpu.SemaphoreType.DMA((3,)),
            pltpu.SemaphoreType.DMA((5,)),
            pltpu.SemaphoreType.DMA((5,)),
            pltpu.SemaphoreType.REGULAR,
            pltpu.SemaphoreType.REGULAR((2,)),
        ],
        compiler_params=pltpu.CompilerParams(collective_id=0, has_side_effects=True),
        name="iterate",
    )(coords, field)
    return pl.pallas_call(
        finish,
        out_shape=(jax.ShapeDtypeStruct((n, points), f32),) * 3,
        in_specs=[vmem] * 4,
        out_specs=(pl.BlockSpec(memory_space=pl.ANY),) * 3,
        scratch_shapes=[pltpu.VMEM((3, n, points), f32), pltpu.SemaphoreType.DMA((3, PIECES))],
        name="finish",
    )(*(pltpu.with_memory_space_constraint(v, pltpu.VMEM) for v in kept))


def solution(mesh):
    return jax.shard_map(
        per_device,
        mesh=mesh,
        in_specs=(P(None, "tiles"), P(None, "tiles"), P(None, "tiles"), P("tiles")),
        out_specs=(P(None, "tiles"), P(None, "tiles"), P(None, "tiles")),
        check_vma=False,
    )
```

```python
import jax
import jax.numpy as jnp
from jax import lax
from jax.experimental import pallas as pl
from jax.experimental.pallas import tpu as pltpu
from jax.sharding import PartitionSpec as P

TILE = 256
BAND = 4
LANE = 128
CHUNK = 64
SILL = 0.2
NUGGET = 1.0
TINY = 16.0 * 1e-12
SCALE = SILL / 256.0
NX, NY, NZ, NC = 4, 4, 16, 2
PLANE = NX * NY * NC
PIECES = 4
GROUP = 4
FIRST = 3
EARLY = 7

f32 = jnp.float32
bf16 = jnp.bfloat16
NT = (((1,), (1,)), ((), ()))
NN = (((1,), (0,)), ((), ()))


def place(me):
    return me // (NZ * NX * NC), (me // (NX * NC)) % NZ, (me // NC) % NX, me % NC


def device(y, z, x, c):
    return (((y % NY) * NZ + z % NZ) * NX + x % NX) * NC + c % NC


def dot(a, b, dims):
    return lax.dot_general(a, b, dims, preferred_element_type=f32)


def lanes(first, count=1):
    return pl.ds(pl.multiple_of(first * LANE, LANE), count * LANE)


def covariance(xc, yc, xr, yr):
    dx = xc - xr
    dy = yc - yr
    q = dx * dx + dy * dy + TINY
    r = q * lax.rsqrt(q)
    s = jnp.maximum(4.0 - r, 0.0)
    s2 = s * s
    return s2 * s2 * (r + 1.0)


def split(v):
    high = v.astype(bf16)
    return high, (v - high.astype(f32)).astype(bf16)


def columns_of(cw, col, tile):
    for d in range(2):
        for h in range(2):
            row = cw[d : d + 1, lanes(tile * 2 + h)]
            col[d, h * LANE : (h + 1) * LANE, :] = jnp.broadcast_to(row, (LANE, LANE)).T


def part(cw, col, tile, j, halves):
    xr = cw[0:1, lanes(tile * 2 + j)]
    yr = cw[1:2, lanes(tile * 2 + j)]
    parts = []
    for h in halves:
        for g in range(h * LANE, (h + 1) * LANE, CHUNK):
            rows = slice(g, g + CHUNK)
            parts.append(split(covariance(col[0, rows, :], col[1, rows, :], xr, yr)))
    return [jnp.concatenate([p[i] for p in parts], 0) for i in (0, 1)]


def block(cw, col, tile, b):
    left, right = [part(cw, col, tile, 2 * b + j, (0, 1)) for j in (0, 1)]
    return [jnp.concatenate([left[i], right[i]], 1) for i in (0, 1)]


def diagonal(cw, col, f2, acc, tile):
    first = part(cw, col, tile, 0, (0,))
    upper = part(cw, col, tile, 1, (0,))
    last = part(cw, col, tile, 1, (1,))
    values = [f2[tile * 2 + j] for j in range(2)]
    values = jnp.concatenate(values + values, 1)
    rows = [jnp.concatenate([first[i], upper[i]], 1) for i in (0, 1)]
    cols = [jnp.concatenate([upper[i], last[i]], 0) for i in (0, 1)]
    acc[:, lanes(tile * 2)] += both(dot(values, jnp.concatenate(rows, 1), NT))
    acc[:, lanes(tile * 2 + 1)] += both(dot(values, jnp.concatenate(cols, 0), NN))


def both(v):
    half = v.shape[0] // 2
    return v[:half] + v[half:]


def row_apply(f2, acc, blocks, tile, b):
    values = [f2[(tile + b) * 2 + j] for j in range(2)]
    out = dot(jnp.concatenate(values + values, 1), jnp.concatenate(blocks, 1), NT)
    acc[:, lanes(tile * 2, 2)] += both(out)


def col_apply(f2, acc, blocks, tile, b):
    values = [f2[tile * 2 + j] for j in range(2)]
    out = dot(jnp.concatenate(values + values, 1), jnp.concatenate(blocks, 0), NN)
    acc[:, lanes((tile + b) * 2, 2)] += both(out)


def order(step, late):
    return jnp.where(
        step < EARLY, step, jnp.where(step < EARLY + BAND, step + late - EARLY, step - BAND)
    )


def kernel(
    tiles,
    c_hbm,
    f_hbm,
    fw,
    image_ref,
    step_ref,
    beta_ref,
    cw,
    f2,
    acc,
    col0,
    col1,
    halo_c,
    halo_f,
    back,
    mine_ref,
    slots1,
    total1,
    slots2,
    load_sem,
    send_sem,
    recv_sem,
    near_sem,
    far_sem,
):
    n = f_hbm.shape[0]
    points = tiles * TILE
    rim = BAND * TILE
    me = lax.axis_index("tiles")
    count = NX * NY * NZ * NC
    y, z, x, c = place(me)
    right, left = (me + 1) % count, (me + count - 1) % count
    other = 1 - c

    load_c = pltpu.make_async_copy(c_hbm, cw.at[:, 0:points], load_sem.at[0])
    load_c.start()
    first = (FIRST + BAND) * TILE
    spans = ((0, first), (first, points))
    load_f = []
    for i, (begin, end) in enumerate(spans):
        at = slice(begin, end)
        load_f.append(pltpu.make_async_copy(f_hbm.at[:, at], fw.at[:, at], load_sem.at[1 + i]))
        load_f[-1].start()

    near = [left, right, device(y, z, x, other)]
    for dy, dz, dx in ((0, 0, 1), (0, 0, -1), (0, 1, 0), (0, -1, 0), (1, 0, 0), (-1, 0, 0)):
        for core in (c, other):
            near.append(device(y + dy, z + dz + NZ, x + dx + NX, core) if dy == 0 else device(y + dy + NY, z, x, core))
    barrier = pltpu.get_barrier_semaphore()
    for target in near:
        pl.semaphore_signal(barrier, inc=1, device_id=(target,))

    halo_copies = [
        pltpu.make_async_remote_copy(
            src_ref=src.at[:, 0:rim],
            dst_ref=dst,
            send_sem=send_sem.at[i],
            recv_sem=recv_sem.at[i],
            device_id=(left,),
        )
        for i, (src, dst) in enumerate(((c_hbm, halo_c), (f_hbm, halo_f)))
    ]
    back_copy = pltpu.make_async_remote_copy(
        src_ref=acc.at[:, points : points + rim],
        dst_ref=back,
        send_sem=send_sem.at[2],
        recv_sem=recv_sem.at[2],
        device_id=(right,),
    )

    def wait_near():
        pl.semaphore_wait(barrier, len(near))
        for copy in halo_copies:
            copy.start()
        for target in near:
            pl.semaphore_signal(near_sem, inc=1, device_id=(target,))

    spread = [device(y, z, x + 2, c), device(y + 2, z, x, c), device(y, z + 2, x, c), device(y, z + NZ - 2, x, c)]
    spread_far = [device(y, z + 4, x, c), device(y, z + NZ - 4, x, c)]

    def wait_two():
        pl.semaphore_wait(near_sem, len(near))
        for i, target in enumerate(spread):
            pl.semaphore_signal(far_sem.at[0], inc=1, device_id=(target,))

    def wait_four():
        pl.semaphore_wait(far_sem.at[0], len(spread))
        for target in spread_far:
            pl.semaphore_signal(far_sem.at[1], inc=1, device_id=(target,))

    def wait_eight():
        pl.semaphore_wait(far_sem.at[1], len(spread_far))

    acc[...] = jnp.zeros_like(acc)
    load_c.wait()
    cw[:, 0:points] = cw[:, 0:points] * 4.0
    columns_of(cw, col0, 0)
    cols = (col0, col1)
    def take(span):
        begin, end = spans[span]
        load_f[span].wait()
        for j in range(begin // LANE, end // LANE):
            high, low = split(fw[:, j * LANE : (j + 1) * LANE])
            f2[j, 0:n, :] = high
            f2[j, n : 2 * n, :] = low

    take(0)

    late = tiles - BAND

    last = tiles - 1

    def strips(start, number, odd=0):
        places = [order(jnp.minimum(start + k, last), late) for k in range(number + 1)]
        for g in range(number):
            now, following = places[g], places[g + 1]
            for b in (*range(1, BAND + 1), 0):
                if b == 0:
                    diagonal(cw, cols[(odd + g) % 2], f2, acc, now)
                    columns_of(cw, cols[(odd + g + 1) % 2], following)
                    continue
                blocks = block(cw, cols[(odd + g) % 2], now, b)
                row_apply(f2, acc, blocks, now, b)
                col_apply(f2, acc, blocks, now, b)

    strips(0, 1)
    wait_near()
    strips(1, FIRST - 1, 1)
    passes = (tiles - FIRST) // GROUP
    rest = tiles - FIRST - passes * GROUP

    @pl.loop(0, passes)
    def _(i):
        start = FIRST + i * GROUP

        @pl.when(i == 0)
        def _():
            take(1)

        @pl.when(start == EARLY)
        def _():
            wait_two()
            for copy in halo_copies:
                copy.wait()
            cw[:, points : points + rim] = halo_c[...] * 4.0
            for j in range(rim // LANE):
                high, low = split(halo_f[:, j * LANE : (j + 1) * LANE])
                f2[points // LANE + j, 0:n, :] = high
                f2[points // LANE + j, n : 2 * n, :] = low

        @pl.when(start == EARLY + BAND)
        def _():
            back_copy.start()
            wait_four()

        strips(start, GROUP, FIRST % 2)

    strips(tiles - rest, rest, (tiles - rest) % 2)
    sums = [jnp.zeros((n, LANE), f32) for _ in range(3)]
    for j in [*range(rim // LANE, points // LANE), *range(rim // LANE)]:
        if j == 0:
            back_copy.wait()
        at = slice(j * LANE, (j + 1) * LANE)
        field = fw[:, at]
        applied = acc[:, at]
        if j < rim // LANE:
            applied = applied + back[:, at]
        image = applied * SCALE + NUGGET * field
        image_ref[:, at] = image
        sums = [sums[0] + field * field, sums[1] + field * image, sums[2] + image * image]

    def over_lanes(v):
        return jnp.sum(v.T, axis=0, keepdims=True)

    mine = jnp.concatenate(
        [
            over_lanes(jnp.concatenate([sums[0], sums[1]], 0)),
            over_lanes(jnp.concatenate([sums[2], sums[2]], 0)),
        ],
        0,
    )

    def gather_sum(values, source, slots, here, members, sems):
        source[...] = values
        slots[here] = values
        copies = []
        for member, target in members:
            copies.append(
                pltpu.make_async_remote_copy(
                    src_ref=source,
                    dst_ref=slots.at[here],
                    send_sem=send_sem.at[sems],
                    recv_sem=recv_sem.at[sems],
                    device_id=(target,),
                )
            )
        for copy in copies:
            copy.start()
        others = slots.at[pl.ds(0, len(members))]
        pltpu.make_async_copy(others, others, recv_sem.at[sems]).wait()
        pltpu.make_async_copy(others, others, send_sem.at[sems]).wait()
        terms = [slots[k] for k in range(len(members) + 1)]
        while len(terms) > 1:
            terms = [a + b for a, b in zip(terms[::2], terms[1::2])]
        return terms[0]

    in_plane = (y * NX + x) * NC + c
    plane = []
    for dy, dx, core in sorted(
        ((a, b, e) for a in range(NY) for b in range(NX) for e in range(NC)),
        key=lambda m: -(min(m[0], NY - m[0]) + min(m[1], NX - m[1]) + m[2]),
    ):
        if (dy, dx, core) != (0, 0, 0):
            at = ((y + dy) % NY, (x + dx) % NX, (c + core) % NC)
            plane.append(((at[0] * NX + at[1]) * NC + at[2], device(at[0], z, at[1], at[2])))
    total = gather_sum(mine, mine_ref, slots1, in_plane, plane, 3)
    line = []
    for k in sorted(range(1, NZ), key=lambda k: -min(k, NZ - k)):
        line.append(((z + k) % NZ, device(y, z + k, x, c)))
    wait_eight()
    total = gather_sum(total, total1, slots2, z, line, 4)

    def columns(row):
        return jnp.broadcast_to(row, (LANE, LANE)).T

    first, second = columns(total[0:1]), columns(total[1:2])
    start_sum, curvature, square = first[:n], first[n:], second[:n]
    step = start_sum / curvature
    new_sum = start_sum - 2.0 * step * curvature + step * step * square
    step_ref[...] = step
    beta_ref[...] = new_sum / start_sum


def finish(field_ref, image_ref, step_ref, beta_ref, solution_hbm, residual_hbm, direction_hbm, made, sem):
    points = field_ref.shape[1]
    size = points // PIECES
    step, beta = step_ref[...], beta_ref[...]
    copies = []
    for p in range(PIECES):
        for j in range(p * size, (p + 1) * size, LANE):
            at = slice(j, j + LANE)
            field = field_ref[:, at]
            residual = field - step * image_ref[:, at]
            made[0, :, at] = step * field
            made[1, :, at] = residual
            made[2, :, at] = residual + beta * field
        at = slice(p * size, (p + 1) * size)
        for i, ref in enumerate((solution_hbm, residual_hbm, direction_hbm)):
            copy = pltpu.make_async_copy(made.at[i, :, at], ref.at[:, at], sem.at[i, p])
            copy.start()
            copies.append(copy)
    for copy in copies:
        copy.wait()


def per_device(coords, field, pair_tiles, pair_count):
    n, points = field.shape
    tiles = points // TILE
    rim = BAND * TILE
    wide = points + rim
    vmem = pl.BlockSpec(memory_space=pltpu.VMEM)
    whole, column = pltpu.VMEM((n, points), f32), pltpu.VMEM((n, LANE), f32)
    kept = pl.pallas_call(
        lambda *refs: kernel(tiles, *refs),
        out_shape=(whole, whole, column, column),
        in_specs=[pl.BlockSpec(memory_space=pl.ANY)] * 2,
        out_specs=(vmem,) * 4,
        scratch_shapes=[
            pltpu.VMEM((2, wide), f32),
            pltpu.VMEM((wide // LANE, 2 * n, LANE), bf16),
            pltpu.VMEM((n, wide), f32),
            pltpu.VMEM((2, TILE, LANE), f32),
            pltpu.VMEM((2, TILE, LANE), f32),
            pltpu.VMEM((2, rim), f32),
            pltpu.VMEM((n, rim), f32),
            pltpu.VMEM((n, rim), f32),
            pltpu.VMEM((2, LANE), f32),
            pltpu.VMEM((PLANE, 2, LANE), f32),
            pltpu.VMEM((2, LANE), f32),
            pltpu.VMEM((NZ, 2, LANE), f32),
            pltpu.SemaphoreType.DMA((3,)),
            pltpu.SemaphoreType.DMA((5,)),
            pltpu.SemaphoreType.DMA((5,)),
            pltpu.SemaphoreType.REGULAR,
            pltpu.SemaphoreType.REGULAR((2,)),
        ],
        compiler_params=pltpu.CompilerParams(collective_id=0, has_side_effects=True),
        name="iterate",
    )(coords, field)
    return pl.pallas_call(
        finish,
        out_shape=(jax.ShapeDtypeStruct((n, points), f32),) * 3,
        in_specs=[vmem] * 4,
        out_specs=(pl.BlockSpec(memory_space=pl.ANY),) * 3,
        scratch_shapes=[pltpu.VMEM((3, n, points), f32), pltpu.SemaphoreType.DMA((3, PIECES))],
        name="finish",
    )(*(pltpu.with_memory_space_constraint(v, pltpu.VMEM) for v in kept))


def solution(mesh):
    return jax.shard_map(
        per_device,
        mesh=mesh,
        in_specs=(P(None, "tiles"), P(None, "tiles"), P(None, "tiles"), P("tiles")),
        out_specs=(P(None, "tiles"), P(None, "tiles"), P(None, "tiles")),
        check_vma=False,
    )
```

```python
import jax
import jax.numpy as jnp
from jax import lax
from jax.experimental import pallas as pl
from jax.experimental.pallas import tpu as pltpu
from jax.sharding import PartitionSpec as P

TILE = 256
BAND = 4
LANE = 128
CHUNK = 64
SILL = 0.2
NUGGET = 1.0
TINY = 16.0 * 1e-12
SCALE = SILL / 256.0
NX, NY, NZ, NC = 4, 4, 16, 2
PLANE = NX * NY * NC
PIECES = 4
GROUP = 4
FIRST = 3

f32 = jnp.float32
bf16 = jnp.bfloat16
NT = (((1,), (1,)), ((), ()))
NN = (((1,), (0,)), ((), ()))


def place(me):
    return me // (NZ * NX * NC), (me // (NX * NC)) % NZ, (me // NC) % NX, me % NC


def device(y, z, x, c):
    return (((y % NY) * NZ + z % NZ) * NX + x % NX) * NC + c % NC


def dot(a, b, dims):
    return lax.dot_general(a, b, dims, preferred_element_type=f32)


def lanes(first, count=1):
    return pl.ds(pl.multiple_of(first * LANE, LANE), count * LANE)


def covariance(xc, yc, xr, yr):
    dx = xc - xr
    dy = yc - yr
    q = dx * dx + dy * dy + TINY
    r = q * lax.rsqrt(q)
    s = jnp.maximum(4.0 - r, 0.0)
    s2 = s * s
    return s2 * s2 * (r + 1.0)


def split(v):
    high = v.astype(bf16)
    return high, (v - high.astype(f32)).astype(bf16)


def columns_of(cw, col, tile):
    for d in range(2):
        for h in range(2):
            row = cw[d : d + 1, lanes(tile * 2 + h)]
            col[d, h * LANE : (h + 1) * LANE, :] = jnp.broadcast_to(row, (LANE, LANE)).T


def part(cw, col, tile, j, halves):
    xr = cw[0:1, lanes(tile * 2 + j)]
    yr = cw[1:2, lanes(tile * 2 + j)]
    parts = []
    for h in halves:
        for g in range(h * LANE, (h + 1) * LANE, CHUNK):
            rows = slice(g, g + CHUNK)
            parts.append(split(covariance(col[0, rows, :], col[1, rows, :], xr, yr)))
    return [jnp.concatenate([p[i] for p in parts], 0) for i in (0, 1)]


def block(cw, col, tile, b):
    left, right = [part(cw, col, tile, 2 * b + j, (0, 1)) for j in (0, 1)]
    return [jnp.concatenate([left[i], right[i]], 1) for i in (0, 1)]


def diagonal(cw, col, f2, acc, tile):
    first = part(cw, col, tile, 0, (0,))
    upper = part(cw, col, tile, 1, (0,))
    last = part(cw, col, tile, 1, (1,))
    values = [f2[tile * 2 + j] for j in range(2)]
    values = jnp.concatenate(values + values, 1)
    rows = [jnp.concatenate([first[i], upper[i]], 1) for i in (0, 1)]
    cols = [jnp.concatenate([upper[i], last[i]], 0) for i in (0, 1)]
    acc[:, lanes(tile * 2)] += both(dot(values, jnp.concatenate(rows, 1), NT))
    acc[:, lanes(tile * 2 + 1)] += both(dot(values, jnp.concatenate(cols, 0), NN))


def both(v):
    half = v.shape[0] // 2
    return v[:half] + v[half:]


def row_apply(f2, acc, blocks, tile, b):
    values = [f2[(tile + b) * 2 + j] for j in range(2)]
    out = dot(jnp.concatenate(values + values, 1), jnp.concatenate(blocks, 1), NT)
    acc[:, lanes(tile * 2, 2)] += both(out)


def col_apply(f2, acc, blocks, tile, b):
    values = [f2[tile * 2 + j] for j in range(2)]
    out = dot(jnp.concatenate(values + values, 1), jnp.concatenate(blocks, 0), NN)
    acc[:, lanes((tile + b) * 2, 2)] += both(out)


def kernel(
    tiles,
    c_hbm,
    f_hbm,
    fw,
    image_ref,
    step_ref,
    beta_ref,
    cw,
    f2,
    acc,
    col0,
    col1,
    halo_c,
    halo_f,
    back,
    kept,
    mine_ref,
    slots1,
    total1,
    slots2,
    load_sem,
    send_sem,
    recv_sem,
    near_sem,
    far_sem,
):
    n = f_hbm.shape[0]
    points = tiles * TILE
    rim = BAND * TILE
    me = lax.axis_index("tiles")
    count = NX * NY * NZ * NC
    y, z, x, c = place(me)
    right, left = (me + 1) % count, (me + count - 1) % count
    other = 1 - c

    load_c = pltpu.make_async_copy(c_hbm, cw.at[:, 0:points], load_sem.at[0])
    load_c.start()
    first = (FIRST + BAND) * TILE
    spans = ((0, first), (first, points))
    load_f = []
    for i, (begin, end) in enumerate(spans):
        at = slice(begin, end)
        load_f.append(pltpu.make_async_copy(f_hbm.at[:, at], fw.at[:, at], load_sem.at[1 + i]))
        load_f[-1].start()

    near = [left, right, device(y, z, x, other)]
    for dy, dz, dx in ((0, 0, 1), (0, 0, -1), (0, 1, 0), (0, -1, 0), (1, 0, 0), (-1, 0, 0)):
        for core in (c, other):
            near.append(device(y + dy, z + dz + NZ, x + dx + NX, core) if dy == 0 else device(y + dy + NY, z, x, core))
    barrier = pltpu.get_barrier_semaphore()
    for target in near:
        pl.semaphore_signal(barrier, inc=1, device_id=(target,))

    halo_copies = [
        pltpu.make_async_remote_copy(
            src_ref=src.at[:, 0:rim],
            dst_ref=dst,
            send_sem=send_sem.at[i],
            recv_sem=recv_sem.at[i],
            device_id=(left,),
        )
        for i, (src, dst) in enumerate(((c_hbm, halo_c), (f_hbm, halo_f)))
    ]
    back_copy = pltpu.make_async_remote_copy(
        src_ref=acc.at[:, points : points + rim],
        dst_ref=back,
        send_sem=send_sem.at[2],
        recv_sem=recv_sem.at[2],
        device_id=(right,),
    )

    def wait_near():
        pl.semaphore_wait(barrier, len(near))
        for copy in halo_copies:
            copy.start()
        for target in near:
            pl.semaphore_signal(near_sem, inc=1, device_id=(target,))

    spread = [device(y, z, x + 2, c), device(y + 2, z, x, c), device(y, z + 2, x, c), device(y, z + NZ - 2, x, c)]
    spread_far = [device(y, z + 4, x, c), device(y, z + NZ - 4, x, c)]

    def wait_two():
        pl.semaphore_wait(near_sem, len(near))
        for i, target in enumerate(spread):
            pl.semaphore_signal(far_sem.at[0], inc=1, device_id=(target,))

    def wait_four():
        pl.semaphore_wait(far_sem.at[0], len(spread))
        for target in spread_far:
            pl.semaphore_signal(far_sem.at[1], inc=1, device_id=(target,))

    def wait_eight():
        pl.semaphore_wait(far_sem.at[1], len(spread_far))

    acc[...] = jnp.zeros_like(acc)
    load_c.wait()
    cw[:, 0:points] = cw[:, 0:points] * 4.0
    columns_of(cw, col0, 0)
    cols = (col0, col1)
    def take(span):
        begin, end = spans[span]
        load_f[span].wait()
        for j in range(begin // LANE, end // LANE):
            high, low = split(fw[:, j * LANE : (j + 1) * LANE])
            f2[j, 0:n, :] = high
            f2[j, n : 2 * n, :] = low

    take(0)

    late = tiles - BAND


    def strips(places, odd=0, over=None):
        for g in range(len(places) - 1):
            now, following = places[g], places[g + 1]
            for b in (*range(1, BAND + 1), 0):
                if b == 0:
                    diagonal(cw, cols[(odd + g) % 2], f2, acc, now)
                    columns_of(cw, cols[(odd + g + 1) % 2], following)
                    continue
                blocks = block(cw, cols[(odd + g) % 2], now, b)
                if over is not None and now + b >= tiles:
                    for i in (0, 1):
                        for h in (0, 1):
                            kept[len(over), i, h, :, :] = blocks[i][:, h * LANE : (h + 1) * LANE]
                    over.append((now, b))
                else:
                    row_apply(f2, acc, blocks, now, b)
                col_apply(f2, acc, blocks, now, b)

    strips([0, 1])
    wait_near()
    take(1)
    strips([1, 2, late], 1)
    halo_copies[0].wait()
    cw[:, points : points + rim] = halo_c[...] * 4.0
    over = []
    strips([*range(late, tiles), FIRST], FIRST % 2, over)
    back_copy.start()

    @pl.loop(0, (late - FIRST) // GROUP)
    def _(i):
        @pl.when(i == 0)
        def _():
            wait_two()

        @pl.when(i == 1)
        def _():
            wait_four()

        start = FIRST + i * GROUP
        strips([start + k for k in range(GROUP + 1)], (FIRST + BAND) % 2)

    halo_copies[1].wait()
    for j in range(rim // LANE):
        high, low = split(halo_f[:, j * LANE : (j + 1) * LANE])
        f2[points // LANE + j, 0:n, :] = high
        f2[points // LANE + j, n : 2 * n, :] = low
    for k, (tile, b) in enumerate(over):
        row_apply(f2, acc, [jnp.concatenate([kept[k, i, 0], kept[k, i, 1]], 1) for i in (0, 1)], tile, b)
    rest = (late - FIRST) % GROUP
    strips(list(range(late - rest, late + 1)), (FIRST + BAND) % 2)

    sums = [jnp.zeros((n, LANE), f32) for _ in range(3)]
    for j in [*range(rim // LANE, points // LANE), *range(rim // LANE)]:
        if j == 0:
            back_copy.wait()
        at = slice(j * LANE, (j + 1) * LANE)
        field = fw[:, at]
        applied = acc[:, at]
        if j < rim // LANE:
            applied = applied + back[:, at]
        image = applied * SCALE + NUGGET * field
        image_ref[:, at] = image
        sums = [sums[0] + field * field, sums[1] + field * image, sums[2] + image * image]

    def over_lanes(v):
        return jnp.sum(v.T, axis=0, keepdims=True)

    mine = jnp.concatenate(
        [
            over_lanes(jnp.concatenate([sums[0], sums[1]], 0)),
            over_lanes(jnp.concatenate([sums[2], sums[2]], 0)),
        ],
        0,
    )

    def gather_sum(values, source, slots, here, members, sems):
        source[...] = values
        slots[here] = values
        copies = []
        for member, target in members:
            copies.append(
                pltpu.make_async_remote_copy(
                    src_ref=source,
                    dst_ref=slots.at[here],
                    send_sem=send_sem.at[sems],
                    recv_sem=recv_sem.at[sems],
                    device_id=(target,),
                )
            )
        for copy in copies:
            copy.start()
        others = slots.at[pl.ds(0, len(members))]
        pltpu.make_async_copy(others, others, recv_sem.at[sems]).wait()
        pltpu.make_async_copy(others, others, send_sem.at[sems]).wait()
        terms = [slots[k] for k in range(len(members) + 1)]
        while len(terms) > 1:
            terms = [a + b for a, b in zip(terms[::2], terms[1::2])]
        return terms[0]

    in_plane = (y * NX + x) * NC + c
    plane = []
    for dy, dx, core in sorted(
        ((a, b, e) for a in range(NY) for b in range(NX) for e in range(NC)),
        key=lambda m: -(min(m[0], NY - m[0]) + min(m[1], NX - m[1]) + m[2]),
    ):
        if (dy, dx, core) != (0, 0, 0):
            at = ((y + dy) % NY, (x + dx) % NX, (c + core) % NC)
            plane.append(((at[0] * NX + at[1]) * NC + at[2], device(at[0], z, at[1], at[2])))
    total = gather_sum(mine, mine_ref, slots1, in_plane, plane, 3)
    line = []
    for k in sorted(range(1, NZ), key=lambda k: -min(k, NZ - k)):
        line.append(((z + k) % NZ, device(y, z + k, x, c)))
    wait_eight()
    total = gather_sum(total, total1, slots2, z, line, 4)

    def columns(row):
        return jnp.broadcast_to(row, (LANE, LANE)).T

    first, second = columns(total[0:1]), columns(total[1:2])
    start_sum, curvature, square = first[:n], first[n:], second[:n]
    step = start_sum / curvature
    new_sum = start_sum - 2.0 * step * curvature + step * step * square
    step_ref[...] = step
    beta_ref[...] = new_sum / start_sum


def finish(field_ref, image_ref, step_ref, beta_ref, solution_hbm, residual_hbm, direction_hbm, made, sem):
    points = field_ref.shape[1]
    size = points // PIECES
    step, beta = step_ref[...], beta_ref[...]
    copies = []
    for p in range(PIECES):
        for j in range(p * size, (p + 1) * size, LANE):
            at = slice(j, j + LANE)
            field = field_ref[:, at]
            residual = field - step * image_ref[:, at]
            made[0, :, at] = step * field
            made[1, :, at] = residual
            made[2, :, at] = residual + beta * field
        at = slice(p * size, (p + 1) * size)
        for i, ref in enumerate((solution_hbm, residual_hbm, direction_hbm)):
            copy = pltpu.make_async_copy(made.at[i, :, at], ref.at[:, at], sem.at[i, p])
            copy.start()
            copies.append(copy)
    for copy in copies:
        copy.wait()


def per_device(coords, field, pair_tiles, pair_count):
    n, points = field.shape
    tiles = points // TILE
    rim = BAND * TILE
    wide = points + rim
    vmem = pl.BlockSpec(memory_space=pltpu.VMEM)
    whole, column = pltpu.VMEM((n, points), f32), pltpu.VMEM((n, LANE), f32)
    kept = pl.pallas_call(
        lambda *refs: kernel(tiles, *refs),
        out_shape=(whole, whole, column, column),
        in_specs=[pl.BlockSpec(memory_space=pl.ANY)] * 2,
        out_specs=(vmem,) * 4,
        scratch_shapes=[
            pltpu.VMEM((2, wide), f32),
            pltpu.VMEM((wide // LANE, 2 * n, LANE), bf16),
            pltpu.VMEM((n, wide), f32),
            pltpu.VMEM((2, TILE, LANE), f32),
            pltpu.VMEM((2, TILE, LANE), f32),
            pltpu.VMEM((2, rim), f32),
            pltpu.VMEM((n, rim), f32),
            pltpu.VMEM((n, rim), f32),
            pltpu.VMEM((BAND * (BAND + 1) // 2, 2, 2, TILE, LANE), bf16),
            pltpu.VMEM((2, LANE), f32),
            pltpu.VMEM((PLANE, 2, LANE), f32),
            pltpu.VMEM((2, LANE), f32),
            pltpu.VMEM((NZ, 2, LANE), f32),
            pltpu.SemaphoreType.DMA((3,)),
            pltpu.SemaphoreType.DMA((5,)),
            pltpu.SemaphoreType.DMA((5,)),
            pltpu.SemaphoreType.REGULAR,
            pltpu.SemaphoreType.REGULAR((2,)),
        ],
        compiler_params=pltpu.CompilerParams(collective_id=0, has_side_effects=True),
        name="iterate",
    )(coords, field)
    return pl.pallas_call(
        finish,
        out_shape=(jax.ShapeDtypeStruct((n, points), f32),) * 3,
        in_specs=[vmem] * 4,
        out_specs=(pl.BlockSpec(memory_space=pl.ANY),) * 3,
        scratch_shapes=[pltpu.VMEM((3, n, points), f32), pltpu.SemaphoreType.DMA((3, PIECES))],
        name="finish",
    )(*(pltpu.with_memory_space_constraint(v, pltpu.VMEM) for v in kept))


def solution(mesh):
    return jax.shard_map(
        per_device,
        mesh=mesh,
        in_specs=(P(None, "tiles"), P(None, "tiles"), P(None, "tiles"), P("tiles")),
        out_specs=(P(None, "tiles"), P(None, "tiles"), P(None, "tiles")),
        check_vma=False,
    )
```
